256 devices in a mesh: row: 16 (over y_lo, x, core), team: 16 (over y_hi, z).
Axes of the slice: x: 4, y: 4 (y_hi: 2, y_lo: 2; y = y_hi * 2 + y_lo), z: 8, core: 2. Of those that a mesh axis runs over, the one named last changes fastest.
Arguments:
- features: bfloat16 [32768, 512], P('row'), may hold values from -6 to 6
- weight: bfloat16 [512, 512], replicated, may hold values from -0.25 to 0.25
- table: bfloat16 [8, 512], replicated, may hold values from -5 to 5
- labels: int32 [32768], P('row'), may hold values from 0 to 7
- label_mask: int32 [32768], P('row'), may hold values 0 or 1
- block_vals: bfloat16 [16, 16, 16, 128, 128], P('row', 'team'), may hold values from -0.25 to 0.25
- block_row: int32 [16, 16, 16], P('row', 'team'), may hold values from 0 to 15, as said below
- block_col: int32 [16, 16, 16], P('row', 'team'), may hold values from 0 to 15
- block_count: int32 [16, 16], P('row', 'team'), may hold values from 1 to 16, as said below
Outputs:
- output: bfloat16 [32768, 512], P(('row', 'team'))
- grad_weight: float32 [512, 512], replicated
- grad_features: bfloat16 [16, 2048, 512], P('team', 'row')
The draws below stay inside these ranges and needn't reach their ends.
Inputs may be any that keep to these rules, and one draw needn't show every extreme that they name: Within one [r, t] list the pairs (block_row, block_col) of all 16 slots are distinct. Only the first block_count[r, t] slots of a list are live; some [r, t] has exactly 16 live slots in every draw.
All inputs are finite; a program needn't handle non-finite values. No bound on the sum of `label_mask` on one device may be relied on, other than what follows from the above.
Results may differ from the reference program's by a relative error of at most 0.0059.
Values may be sent and summed in bfloat16 or wider, within the bound.
A program may use at most 64 MiB of HBM per device.

```python
import math
import jax
import jax.numpy as jnp
from jax import lax

F = 512
CL = 8
SB = 16
KMAX = 16
PANEL_SLABS = 1
SLAB = 2048
NODES = 32768
N_ROW = 16
N_TEAM = 16


def block_layout(key):
    device_keys = jax.random.split(key, N_ROW * N_TEAM)
    shuffled = jax.vmap(lambda one_key: jax.random.permutation(one_key, PANEL_SLABS * SB * SB))(device_keys)
    return shuffled[:, :KMAX].reshape(N_ROW, N_TEAM, KMAX).astype(jnp.int32)


def draw_block_row(key, part):
    layout = block_layout(jax.random.fold_in(key, 7))
    return (layout // (PANEL_SLABS * SB)).astype(jnp.int32)


def draw_block_col(key, part):
    layout = block_layout(jax.random.fold_in(key, 7))
    return (layout % (PANEL_SLABS * SB)).astype(jnp.int32)


def draw_block_count(key, part):
    first_key, second_key, third_key = jax.random.split(jax.random.fold_in(key, 11), 3)
    devices = N_ROW * N_TEAM
    counts = jax.random.randint(first_key, (devices,), max(1, KMAX // 8), KMAX // 2 + 1)
    first_full = jax.random.randint(second_key, (), 0, devices)
    second_full = jax.random.randint(third_key, (), 0, devices)
    places = jnp.arange(devices, dtype=jnp.int32)
    counts = jnp.where((places == first_full) | (places == second_full), KMAX, counts)
    return counts.reshape(N_ROW, N_TEAM).astype(jnp.int32)


def touch_ends(drawn, stream_key, smallest, top_value):
    longest = drawn.shape.index(max(drawn.shape))
    spots = []
    for shift in (0, 1):
        where = [jax.random.randint(jax.random.fold_in(stream_key, axis), (), 0, length) for axis, length in enumerate(drawn.shape)]
        where[longest] = (where[longest] + shift) % drawn.shape[longest]
        spots.append(tuple(where))
    return drawn.at[spots[0]].set(smallest).at[spots[1]].set(top_value)


def levels(stream_key, dims, cuts, low, high):
    loudness, own = 1.0, jax.random.fold_in(stream_key, 6)
    for dim, shards_of in cuts:
        heights = jnp.exp(jax.random.uniform(jax.random.fold_in(own, dim), (shards_of,), jnp.float32, low / len(cuts), high / len(cuts)))
        loudness = loudness * jnp.repeat(heights, dims[dim] // shards_of).reshape([-1 if axis == dim else 1 for axis in range(len(dims))])
    return loudness


def centred(key, shape, deviation, reach, shards=(), kind=jnp.bfloat16):
    entries = jax.random.normal(key, shape, jnp.float32) * deviation
    if len(shards) > 0:
        entries = levels(key, shape, shards, -0.22, 0.18) * entries
    return jnp.clip(entries, min=-reach, max=reach).astype(kind)


def setup_inputs(seed: int = 0) -> dict:
    key_of = jax.random.split(jax.random.key(seed), 10)
    features = centred(key_of[0], (NODES, F), 1.0, 6.0, ((0, 16),))
    weight = centred(key_of[1], (F, F), F ** -0.5, 0.25)
    table = centred(key_of[2], (CL, F), 1.0, 5.0)
    labels = touch_ends(jax.random.randint(key_of[3], (NODES,), 0, CL), jax.random.fold_in(key_of[3], 1), 0, CL - 1).astype(jnp.int32)
    label_mask = touch_ends((jax.random.randint(key_of[4], (NODES,), 0, 2) < 1).astype(jnp.int32), jax.random.fold_in(key_of[4], 1), 0, 1)
    block_vals = centred(key_of[5], (N_ROW, N_TEAM, KMAX, 128, 128), (32 * KMAX) ** -0.5, 0.25, ((0, 16), (1, 16)))
    block_row = draw_block_row(jax.random.fold_in(key_of[9], 71), 0)
    block_col = draw_block_col(jax.random.fold_in(key_of[9], 71), 0)
    block_count = draw_block_count(jax.random.fold_in(key_of[9], 71), 0)
    return dict(features=features, weight=weight, table=table, labels=labels, label_mask=label_mask, block_vals=block_vals, block_row=block_row, block_col=block_col, block_count=block_count)


def silu_slope(preact):
    sigma = jax.nn.sigmoid(preact)
    return sigma * (1.0 + preact * (1.0 - sigma))

def reference(features, weight, table, labels, label_mask, block_vals, block_row, block_col, block_count):
    feature_width = features.shape[1]
    panel_rows = PANEL_SLABS * SLAB

    def forward_slab(slab_index):

        def team_part(totals, team_index):
            feature_panel = lax.dynamic_slice_in_dim(features, (team_index * panel_rows).astype(jnp.int32), panel_rows, 0)

            def add_block(position, inner):
                col_start = (block_col[slab_index, team_index, position] * 128).astype(jnp.int32)
                row_start = (block_row[slab_index, team_index, position] * 128).astype(jnp.int32)
                source = lax.dynamic_slice_in_dim(feature_panel, col_start, 128, 0)
                product = jnp.dot(block_vals[slab_index, team_index, position], source, preferred_element_type=jnp.float32)
                current = lax.dynamic_slice_in_dim(inner, row_start, 128, 0)
                return lax.dynamic_update_slice_in_dim(inner, current + product, row_start, 0)
            totals = lax.fori_loop(jnp.int32(0), block_count[slab_index, team_index], add_block, totals)
            return (totals, None)
        totals, unused = lax.scan(team_part, jnp.zeros((SLAB, feature_width), jnp.float32), jnp.arange(N_TEAM, dtype=jnp.int32))
        return totals
    agg = lax.map(forward_slab, jnp.arange(N_ROW, dtype=jnp.int32)).reshape(NODES, feature_width).astype(jnp.bfloat16)
    preact = jnp.dot(agg, weight, preferred_element_type=jnp.float32)
    active = jax.nn.silu(preact)
    output = active.astype(jnp.bfloat16)
    target = table.astype(jnp.float32)[labels]
    residual = label_mask.astype(jnp.float32)[:, None] * (active - target)
    grad_pre = (residual * silu_slope(preact)).astype(jnp.bfloat16)
    grad_weight = jnp.dot(agg.T, grad_pre, preferred_element_type=jnp.float32) * (1.0 / math.sqrt(NODES))
    back_rows = jnp.dot(grad_pre, weight.T, preferred_element_type=jnp.float32).astype(jnp.bfloat16)

    def backward_panel(team_index):

        def row_part(totals, slab_index):
            back_slab = lax.dynamic_slice_in_dim(back_rows, (slab_index * SLAB).astype(jnp.int32), SLAB, 0)

            def add_block(position, inner):
                col_start = (block_col[slab_index, team_index, position] * 128).astype(jnp.int32)
                row_start = (block_row[slab_index, team_index, position] * 128).astype(jnp.int32)
                source = lax.dynamic_slice_in_dim(back_slab, row_start, 128, 0)
                product = jnp.dot(block_vals[slab_index, team_index, position].T, source, preferred_element_type=jnp.float32)
                current = lax.dynamic_slice_in_dim(inner, col_start, 128, 0)
                return lax.dynamic_update_slice_in_dim(inner, current + product, col_start, 0)
            totals = lax.fori_loop(jnp.int32(0), block_count[slab_index, team_index], add_block, totals)
            return (totals, None)
        totals, unused = lax.scan(row_part, jnp.zeros((panel_rows, feature_width), jnp.float32), jnp.arange(N_ROW, dtype=jnp.int32))
        return totals
    grad_features = lax.map(backward_panel, jnp.arange(N_TEAM, dtype=jnp.int32)).astype(jnp.bfloat16)
    return (output, grad_weight, grad_features)
```

```python
import functools
import math

import jax
import jax.numpy as jnp
from jax import lax
from jax.experimental import pallas as pl
from jax.experimental.pallas import tpu as pltpu
from jax.sharding import PartitionSpec as P

MESH = pl.DeviceIdType.MESH
BF16 = jnp.bfloat16
F32 = jnp.float32
HALVES = 2
WIDE = 256
PIECE = 64
TREES = ((0, 11), (11, 10), (21, 11))
DEEPEST = 5


def rem(value, size):
    return lax.rem(value, jnp.int32(size))


def div(value, size):
    return lax.div(value, jnp.int32(size))


def remote(src, dst, send_sem, recv_sem, device):
    return pltpu.make_async_remote_copy(
        src_ref=src,
        dst_ref=dst,
        send_sem=send_sem,
        recv_sem=recv_sem,
        device_id=device,
        device_id_type=MESH,
    )


def pick(index, table):
    value = jnp.int32(table[0])
    for position, entry in enumerate(table[1:], 1):
        value = jnp.where(index == position, jnp.int32(entry), value)
    return value


def layer_kernel(
    feat,
    weight,
    table,
    labels,
    mask,
    vals,
    brow,
    bcol,
    bcnt,
    out,
    gw_out,
    gf_out,
    xv,
    vt,
    slots,
    part,
    zs,
    zr,
    ys,
    yr,
    keep,
    gath,
    gw32,
    gwb,
    g1r,
    g1t,
    g2r,
    g3,
    g4,
    sp,
    prx,
    chip,
    xs,
    xr,
    bs,
    br,
    bc_recv,
    bc_send,
    z_send,
    z_recv,
    y_send,
    y_recv,
    ag_send,
    ag_recv,
    gw_send,
    gw_recv,
    p_send,
    p_recv,
    x_send,
    x_recv,
    b_send,
    b_recv,
):
    row = lax.axis_index("row")
    team = lax.axis_index("team")
    core = rem(row, 2)
    x = rem(div(row, 2), 4)
    ylo = div(row, 8)
    z = rem(team, 8)
    yhi = div(team, 8)

    def at_row(new_y, new_x, new_core):
        return ((new_y * 4 + rem(new_x + 4, 4)) * 2 + new_core, team)

    def at_team(new_yhi, new_z):
        return (row, new_yhi * 8 + rem(new_z + 8, 8))

    partner = at_row(ylo, x, 1 - core)
    x_up, x_down = at_row(ylo, x + 1, core), at_row(ylo, x - 1, core)
    y_side = at_row(1 - ylo, x, core)
    z_up, z_down = at_team(yhi, z + 1), at_team(yhi, z - 1)
    y_far = at_team(1 - yhi, z)

    barrier = pltpu.get_barrier_semaphore()

    def greet(d, carry):
        pl.semaphore_signal(
            barrier, inc=1, device_id=(rem(row + d, 16), team), device_id_type=MESH
        )
        pl.semaphore_signal(
            barrier, inc=1, device_id=(row, rem(team + d, 16)), device_id_type=MESH
        )
        return carry

    lax.fori_loop(1, 16, greet, 0)

    root = team
    root_core = rem(root, 2)
    rx = rem(x - rem(div(root, 2), 4) + 4, 4)
    ry = rem(ylo + div(root, 8), 2)
    lead = core == root_core
    is_root = row == root
    pieces = feat.shape[0] // PIECE

    def landed(piece):
        return xv.at[div(piece, 2), pl.ds(pl.multiple_of(rem(piece, 2) * PIECE, PIECE), PIECE)]

    def stage(piece):
        return pltpu.make_async_copy(
            feat.at[pl.ds(pl.multiple_of(piece * PIECE, PIECE), PIECE)],
            landed(piece),
            bc_recv.at[piece],
        )

    @pl.when(is_root)
    def _():
        def begin(piece, carry):
            stage(piece).start()
            return carry

        lax.fori_loop(0, pieces, begin, 0)

    slots[16] = jnp.zeros((128, 512), F32)
    for k in range(16):
        vt[k] = vals[k].T

    pl.semaphore_wait(barrier, 30)

    low = ry == 0
    depths = (
        jnp.where(low, pick(rx, (0, 1, 2, 3)), pick(rx, (5, 2, 3, 4))),
        jnp.where(low, pick(rx, (0, 3, 2, 1)), pick(rx, (5, 4, 3, 2))),
        jnp.where(low, pick(rx, (0, 3, 4, 3)), pick(rx, (1, 2, 3, 2))),
    )
    ups = (
        (low & (rx < 3)) | (~low & (rx > 1)),
        None,
        ~low & (rx < 2),
    )
    downs = (
        None,
        (low & (rx != 1)) | (~low & (rx > 0)),
        ~low & (rx == 0),
    )
    sides = (
        low & ((rx == 1) | (rx == 2)),
        low & (rx == 3),
        (low & (rx == 0)) | (~low & (rx > 0)),
    )

    def hop(piece, way, device):
        ref = landed(piece)
        return remote(ref, ref, bc_send.at[way, piece], bc_recv.at[piece], device)

    def branches(tree):
        return (
            (0, ups[tree], x_up),
            (1, downs[tree], x_down),
            (2, sides[tree], y_side),
            (3, None if tree < 0 else jnp.bool_(True), partner),
        )

    @pl.when(lead)
    def _():
        def beat(tick, carry):
            for tree, (first, number) in enumerate(TREES):
                q = tick - depths[tree]

                @pl.when((q >= 0) & (q < number))
                def _(tree=tree, first=first, q=q):
                    piece = first + q

                    @pl.when(is_root)
                    def _():
                        stage(piece).wait()

                    @pl.when(jnp.logical_not(is_root))
                    def _():
                        hop(piece, 3, partner).wait_recv()

                    for way, condition, device in branches(tree):
                        if condition is None:
                            continue

                        @pl.when(condition)
                        def _(way=way, device=device):
                            hop(piece, way, device).start()

            return carry

        lax.fori_loop(0, 11 + DEEPEST, beat, 0)

        def settle(q, carry):
            for tree, (first, number) in enumerate(TREES):

                @pl.when(q < number)
                def _(tree=tree, first=first):
                    for way, condition, device in branches(tree):
                        if condition is None:
                            continue

                        @pl.when(condition)
                        def _(way=way, device=device):
                            hop(first + q, way, device).wait_send()

            return carry

        lax.fori_loop(0, 11, settle, 0)

    @pl.when(jnp.logical_not(lead))
    def _():
        def arrive(piece, carry):
            hop(piece, 3, partner).wait_recv()
            return carry

        lax.fori_loop(0, pieces, arrive, 0)

    count = bcnt[0]

    def before(ids, k):
        found = jnp.int32(16)
        for other in range(k):
            found = jnp.where(ids[other] == ids[k], jnp.int32(other), found)
        return found

    def final(ids, target):
        found = jnp.int32(16)
        for other in range(16):
            hit = (ids[other] == target) & (jnp.int32(other) < count)
            found = jnp.where(hit, jnp.int32(other), found)
        return found

    for k in range(16):
        product = jnp.dot(vals[k], xv[bcol[k]], preferred_element_type=F32)
        slots[k] = product + slots[before(brow, k)] if k else product
    for s in range(16):
        value = slots[final(brow, s)].astype(BF16)
        for h in range(HALVES):
            part[h, s] = value[:, h * WIDE : (h + 1) * WIDE]

    def block(new_z, rel):
        return rem(yhi + rel, 2) * 8 + rem(new_z + 8, 8)

    ways = ((0, 1, z_up), (1, -1, z_down))

    def z_first(h, way, sign, device):
        return remote(
            part.at[h, block(z + 4, way)],
            zr.at[way, 0, h, way],
            z_send.at[way, 0, h],
            z_recv.at[way, 0, h],
            device,
        )

    def z_hop(h, way, step, device):
        return remote(
            zs.at[way, step, h],
            zr.at[way, step, h],
            z_send.at[way, step, h],
            z_recv.at[way, step, h],
            device,
        )

    for h in range(HALVES):
        for way, sign, device in ways:
            z_first(h, way, sign, device).start()
    for step in range(1, 4):
        for h in range(HALVES):
            for way, sign, device in ways:
                if step == 1:
                    z_first(h, way, sign, device).wait_recv()
                else:
                    z_hop(h, way, step - 1, device).wait_recv()
                for rel in range(2):
                    value = part[h, block(z + sign * (4 - step), rel)]
                    if step > 1 or rel == way:
                        value = (
                            value.astype(F32) + zr[way, step - 1, h, rel].astype(F32)
                        ).astype(BF16)
                    zs[way, step, h, rel] = value
                z_hop(h, way, step, device).start()

    def y_hop(h):
        return remote(ys.at[h], yr.at[h], y_send.at[h], y_recv.at[h], y_far)

    for h in range(HALVES):
        for way, sign, device in ways:
            z_hop(h, way, 3, device).wait_recv()
        sums = [
            part[h, block(z, rel)].astype(F32)
            + zr[0, 3, h, rel].astype(F32)
            + zr[1, 3, h, rel].astype(F32)
            for rel in range(2)
        ]
        ys[h] = sums[1].astype(BF16)
        y_hop(h).start()
        keep[:, h * WIDE : (h + 1) * WIDE] = sums[0]
    for h in range(HALVES):
        y_hop(h).wait_recv()
    agg = jnp.concatenate(
        [
            (keep[:, h * WIDE : (h + 1) * WIDE] + yr[h].astype(F32)).astype(BF16)
            for h in range(HALVES)
        ],
        axis=1,
    )

    preact = jnp.dot(agg, weight[...], preferred_element_type=F32)
    sigma = jax.nn.sigmoid(preact)
    active = preact * sigma
    out[...] = active.astype(BF16)
    label_line = jnp.broadcast_to(labels[pl.ds(team, 1), :], (128, 128))
    classes = lax.broadcasted_iota(jnp.int32, (128, 128), 0)
    onehot = (label_line == classes).astype(F32).T
    spare = jnp.zeros((120, 512), F32)
    wide_table = jnp.concatenate([table[...].astype(F32), spare], axis=0)
    target = jnp.dot(onehot, wide_table, preferred_element_type=F32)
    known = jnp.broadcast_to(mask[pl.ds(team, 1), :], (128, 128)).astype(F32).T
    known = jnp.concatenate([known] * 4, axis=1)
    residual = known * (active - target)
    slope = sigma * (1.0 + preact * (1.0 - sigma))
    grad_pre = (residual * slope).astype(BF16)
    back = lax.dot_general(
        grad_pre, weight[...], (((1,), (1,)), ((), ())), preferred_element_type=F32
    ).astype(BF16)
    gath[team] = back

    def cols(h):
        return pl.ds(h * WIDE, WIDE)

    def ag_hop(step, way, rel, h, device):
        sign = 1 if way == 0 else -1
        origin = block(z - sign * (step - 1), rel)
        ref = gath.at[origin, :, cols(h)]
        return remote(
            ref, ref, ag_send.at[way, step, rel, h], ag_recv.at[way, step, rel, h], device
        )

    def ag_wait(step, way, rel, h, device):
        sign = 1 if way == 0 else -1
        origin = block(z - sign * step, rel)
        ref = gath.at[origin, :, cols(h)]
        remote(
            ref, ref, ag_send.at[way, step, rel, h], ag_recv.at[way, step, rel, h], device
        ).wait_recv()

    def ag_side(h, slot):
        ref = gath.at[slot, :, cols(h)]
        return remote(ref, ref, y_send.at[2 + h], y_recv.at[2 + h], y_far)

    for h in range(HALVES):
        ag_side(h, team).start()
        for way, sign, device in ways:
            ag_hop(1, way, 0, h, device).start()
    gw = lax.dot_general(
        agg, grad_pre, (((0,), (0,)), ((), ())), preferred_element_type=F32
    ).reshape(16, 32, 512)
    gw32[...] = gw
    gwb[...] = gw.astype(BF16)

    def peer_row(d):
        return (rem(row + d, 16), team)

    def peer_team(d):
        return (row, rem(team + d, 16))

    def gw_hop(stage_id, d, receive):
        slot_row = rem(row - d + 16, 16) if receive else row
        slot_team = rem(team - d + 16, 16) if receive else team
        to_row, to_team = rem(row + d, 16), rem(team + d, 16)
        if stage_id == 0:
            src, dst, device = gwb.at[to_row], g1r.at[slot_row], peer_row(d)
        elif stage_id == 1:
            src, dst, device = g1t.at[to_team], g2r.at[slot_team], peer_team(d)
        elif stage_id == 2:
            src, dst, device = g3.at[slot_team], g3.at[slot_team], peer_team(d)
        else:
            src, dst, device = g4.at[slot_row], g4.at[slot_row], peer_row(d)
        return remote(
            src, dst, gw_send.at[stage_id, d], gw_recv.at[stage_id, d], device
        )

    def gw_start(stage_id):
        def one(d, carry):
            gw_hop(stage_id, d, False).start()
            return carry

        lax.fori_loop(1, 16, one, 0)

    def gw_arrive(stage_id):
        def one(d, carry):
            gw_hop(stage_id, d, True).wait_recv()
            return carry

        lax.fori_loop(1, 16, one, 0)

    def gw_stage(stage_id):
        gw_arrive(stage_id)
        if stage_id == 0:

            def one(d, total):
                return total + g1r[rem(row + d, 16)].astype(F32)

            total = lax.fori_loop(1, 16, one, gw32[row])
            for a in range(4):
                for b in range(4):
                    g1t[a * 4 + b] = total[a * 8 : a * 8 + 8, b * 128 : b * 128 + 128]
        elif stage_id == 1:

            def one(d, total):
                return total + g2r[rem(team + d, 16)]

            g3[team] = lax.fori_loop(1, 16, one, g1t[team])
        elif stage_id == 2:
            lines = [
                jnp.concatenate([g3[a * 4 + b] for b in range(4)], axis=1)
                for a in range(4)
            ]
            scale = 1.0 / math.sqrt(32768)
            g4[row] = (jnp.concatenate(lines, axis=0) * scale).astype(BF16)
        if stage_id < 3:
            gw_start(stage_id + 1)

    gw_start(0)
    for h in range(HALVES):
        ag_side(h, rem(team + 8, 16)).wait_recv()
        for way, sign, device in ways:
            ag_hop(1, way, 1, h, device).start()
    for step in range(2, 5):
        for rel in range(2):
            for h in range(HALVES):
                for way, sign, device in ways:
                    ag_wait(step - 1, way, rel, h, device)
                    if step < 4 or rel == way:
                        ag_hop(step, way, rel, h, device).start()
        gw_stage(step - 2)
    for rel in range(2):
        for h in range(HALVES):
            ag_wait(4, rel, rel, h, ways[rel][2])

    for k in range(16):
        product = jnp.dot(vt[k], gath[brow[k]], preferred_element_type=F32)
        slots[k] = product + slots[before(bcol, k)] if k else product
    for s in range(16):
        value = slots[final(bcol, s)].astype(BF16)
        for h in range(HALVES):
            sp[h, s % 2, s // 2] = value[:, h * WIDE : (h + 1) * WIDE]

    def p_hop(h):
        return remote(sp.at[h, 1 - core], prx.at[h], p_send.at[h], p_recv.at[h], partner)

    def chip_block(new_x, rel):
        return rem(ylo + rel, 2) * 4 + rem(new_x + 4, 4)

    x_ways = ((0, 1, x_up), (1, -1, x_down))

    def x_first(h, way, device):
        return remote(
            chip.at[h, chip_block(x + 2, way)],
            xr.at[way, 0, h, way],
            x_send.at[way, 0, h],
            x_recv.at[way, 0, h],
            device,
        )

    def x_hop(h, way, device):
        return remote(
            xs.at[way, h],
            xr.at[way, 1, h],
            x_send.at[way, 1, h],
            x_recv.at[way, 1, h],
            device,
        )

    def b_hop(h):
        return remote(bs.at[h], br.at[h], b_send.at[h], b_recv.at[h], y_side)

    for h in range(HALVES):
        p_hop(h).start()
    for h in range(HALVES):
        p_hop(h).wait_recv()

        def fold(m, carry, h=h):
            chip[h, m] = (sp[h, core, m].astype(F32) + prx[h, m].astype(F32)).astype(BF16)
            return carry

        lax.fori_loop(0, 8, fold, 0)
        for way, sign, device in x_ways:
            x_first(h, way, device).start()
    for h in range(HALVES):
        for way, sign, device in x_ways:
            x_first(h, way, device).wait_recv()
            for rel in range(2):
                value = chip[h, chip_block(x + sign, rel)]
                if rel == way:
                    value = (value.astype(F32) + xr[way, 0, h, rel].astype(F32)).astype(BF16)
                xs[way, h, rel] = value
            x_hop(h, way, device).start()
    for h in range(HALVES):
        for way, sign, device in x_ways:
            x_hop(h, way, device).wait_recv()
        sums = [
            chip[h, chip_block(x, rel)].astype(F32)
            + xr[0, 1, h, rel].astype(F32)
            + xr[1, 1, h, rel].astype(F32)
            for rel in range(2)
        ]
        bs[h] = sums[1].astype(BF16)
        b_hop(h).start()
        keep[:, h * WIDE : (h + 1) * WIDE] = sums[0]
    gw_stage(3)
    for a in range(16):
        gw_out[a * 32 : a * 32 + 32, :] = g4[a].astype(F32)
    for h in range(HALVES):
        b_hop(h).wait_recv()
        gf_out[:, h * WIDE : (h + 1) * WIDE] = (
            keep[:, h * WIDE : (h + 1) * WIDE] + br[h].astype(F32)
        ).astype(BF16)

    for h in range(HALVES):
        for way, sign, device in ways:
            z_first(h, way, sign, device).wait_send()
            for step in range(1, 4):
                z_hop(h, way, step, device).wait_send()
            for rel in range(2):
                for step in range(1, 5):
                    if step < 4 or rel == way:
                        ag_hop(step, way, rel, h, device).wait_send()
        y_hop(h).wait_send()
        ag_side(h, team).wait_send()
        p_hop(h).wait_send()
        b_hop(h).wait_send()
        for way, sign, device in x_ways:
            x_first(h, way, device).wait_send()
            x_hop(h, way, device).wait_send()

    def sent(d, carry):
        for stage_id in range(4):
            gw_hop(stage_id, d, False).wait_send()
        return carry

    lax.fori_loop(1, 16, sent, 0)


def per_device(
    features, weight, table, labels, label_mask, block_vals, block_row, block_col, block_count
):
    vmem = pl.BlockSpec(memory_space=pltpu.VMEM)
    smem = pl.BlockSpec(memory_space=pltpu.SMEM)
    dma = pltpu.SemaphoreType.DMA
    half = (HALVES, 128, WIDE)
    outs = pl.pallas_call(
        layer_kernel,
        out_shape=(
            jax.ShapeDtypeStruct((128, 512), BF16),
            jax.ShapeDtypeStruct((512, 512), F32),
            jax.ShapeDtypeStruct((128, 512), BF16),
        ),
        in_specs=[pl.BlockSpec(memory_space=pl.ANY)] + [vmem] * 5 + [smem] * 3,
        out_specs=(vmem, vmem, vmem),
        scratch_shapes=[
            pltpu.VMEM((16, 128, 512), BF16),
            pltpu.VMEM((16, 128, 128), BF16),
            pltpu.VMEM((17, 128, 512), F32),
            pltpu.VMEM((HALVES, 16, 128, WIDE), BF16),
            pltpu.VMEM((2, 4, HALVES, 2, 128, WIDE), BF16),
            pltpu.VMEM((2, 4, HALVES, 2, 128, WIDE), BF16),
            pltpu.VMEM(half, BF16),
            pltpu.VMEM(half, BF16),
            pltpu.VMEM((128, 512), F32),
            pltpu.VMEM((16, 128, 512), BF16),
            pltpu.VMEM((16, 32, 512), F32),
            pltpu.VMEM((16, 32, 512), BF16),
            pltpu.VMEM((16, 32, 512), BF16),
            pltpu.VMEM((16, 8, 128), F32),
            pltpu.VMEM((16, 8, 128), F32),
            pltpu.VMEM((16, 8, 128), F32),
            pltpu.VMEM((16, 32, 512), BF16),
            pltpu.VMEM((HALVES, 2, 8, 128, WIDE), BF16),
            pltpu.VMEM((HALVES, 8, 128, WIDE), BF16),
            pltpu.VMEM((HALVES, 8, 128, WIDE), BF16),
            pltpu.VMEM((2, HALVES, 2, 128, WIDE), BF16),
            pltpu.VMEM((2, 2, HALVES, 2, 128, WIDE), BF16),
            pltpu.VMEM(half, BF16),
            pltpu.VMEM(half, BF16),
            dma((32,)),
            dma((4, 32)),
            dma((2, 4, HALVES)),
            dma((2, 4, HALVES)),
            dma((4,)),
            dma((4,)),
            dma((2, 5, 2, HALVES)),
            dma((2, 5, 2, HALVES)),
            dma((4, 16)),
            dma((4, 16)),
            dma((HALVES,)),
            dma((HALVES,)),
            dma((2, 2, HALVES)),
            dma((2, 2, HALVES)),
            dma((HALVES,)),
            dma((HALVES,)),
        ],
        compiler_params=pltpu.CompilerParams(collective_id=0, has_side_effects=True),
        name="layer",
    )(
        features,
        weight,
        table,
        labels.reshape(16, 128),
        label_mask.reshape(16, 128),
        block_vals[0, 0],
        block_row[0, 0],
        block_col[0, 0],
        block_count[0],
    )
    output, grad_weight, grad_piece = outs
    return (output, grad_weight, grad_piece[None])


def solution(mesh):
    placed = (
        P("row", None),
        P(),
        P(),
        P("row"),
        P("row"),
        P("row", "team", None, None, None),
        P("row", "team", None),
        P("row", "team", None),
        P("row", "team"),
    )
    return jax.shard_map(
        per_device,
        mesh=mesh,
        in_specs=placed,
        out_specs=(P(("row", "team"), None), P(), P("team", "row", None)),
        check_vma=False,
    )
```

```python
import functools
import math

import jax
import jax.numpy as jnp
from jax import lax
from jax.experimental import pallas as pl
from jax.experimental.pallas import tpu as pltpu
from jax.sharding import PartitionSpec as P

MESH = pl.DeviceIdType.MESH
BF16 = jnp.bfloat16
F32 = jnp.float32
PARTS = 4
WIDE = 128
AG_PARTS = 2
AG_WIDE = 256
PIECE = 32
TREES = ((0, 22), (22, 20), (42, 22))
LONGEST = 22
DEEPEST = 5
LAG = 9


def rem(value, size):
    return lax.rem(value, jnp.int32(size))


def div(value, size):
    return lax.div(value, jnp.int32(size))


def remote(src, dst, send_sem, recv_sem, device):
    return pltpu.make_async_remote_copy(
        src_ref=src,
        dst_ref=dst,
        send_sem=send_sem,
        recv_sem=recv_sem,
        device_id=device,
        device_id_type=MESH,
    )


def pick(index, table):
    value = jnp.int32(table[0])
    for position, entry in enumerate(table[1:], 1):
        value = jnp.where(index == position, jnp.int32(entry), value)
    return value


def layer_kernel(
    feat,
    weight,
    table,
    labels,
    mask,
    vals,
    brow,
    bcol,
    bcnt,
    out,
    gw_out,
    gf_out,
    xv,
    vt,
    slots,
    part,
    zs,
    zr,
    ys,
    yr,
    keep,
    gath,
    gw32,
    gwb,
    g1r,
    g1t,
    g2r,
    g3,
    g4,
    sp,
    prx,
    chip,
    xs,
    xr,
    bs,
    br,
    bc_recv,
    bc_send,
    z_send,
    z_recv,
    y_send,
    y_recv,
    ag_send,
    ag_recv,
    gw_send,
    gw_recv,
    p_send,
    p_recv,
    x_send,
    x_recv,
    b_send,
    b_recv,
):
    row = lax.axis_index("row")
    team = lax.axis_index("team")
    core = rem(row, 2)
    x = rem(div(row, 2), 4)
    ylo = div(row, 8)
    z = rem(team, 8)
    yhi = div(team, 8)

    def at_row(new_y, new_x, new_core):
        return ((new_y * 4 + rem(new_x + 4, 4)) * 2 + new_core, team)

    def at_team(new_yhi, new_z):
        return (row, new_yhi * 8 + rem(new_z + 8, 8))

    partner = at_row(ylo, x, 1 - core)
    x_up, x_down = at_row(ylo, x + 1, core), at_row(ylo, x - 1, core)
    y_side = at_row(1 - ylo, x, core)
    z_up, z_down = at_team(yhi, z + 1), at_team(yhi, z - 1)
    y_far = at_team(1 - yhi, z)

    barrier = pltpu.get_barrier_semaphore()

    def greet(d, carry):
        pl.semaphore_signal(
            barrier, inc=1, device_id=(rem(row + d, 16), team), device_id_type=MESH
        )
        pl.semaphore_signal(
            barrier, inc=1, device_id=(row, rem(team + d, 16)), device_id_type=MESH
        )
        return carry

    lax.fori_loop(1, 16, greet, 0)

    root = team
    root_core = rem(root, 2)
    rx = rem(x - rem(div(root, 2), 4) + 4, 4)
    ry = rem(ylo + div(root, 8), 2)
    lead = core == root_core
    is_root = row == root
    pieces = feat.shape[0] // PIECE

    def landed(piece):
        return xv.at[
            div(piece, 128 // PIECE),
            pl.ds(pl.multiple_of(rem(piece, 128 // PIECE) * PIECE, PIECE), PIECE),
        ]

    def stage(piece):
        return pltpu.make_async_copy(
            feat.at[pl.ds(pl.multiple_of(piece * PIECE, PIECE), PIECE)],
            landed(piece),
            bc_recv.at[piece],
        )

    @pl.when(is_root)
    def _():
        def begin(piece, carry):
            stage(piece).start()
            return carry

        lax.fori_loop(0, pieces, begin, 0)

    slots[16] = jnp.zeros((128, 512), F32)
    for k in range(16):
        vt[k] = vals[k].T

    pl.semaphore_wait(barrier, 30)

    low = ry == 0
    depths = (
        jnp.where(low, pick(rx, (0, 1, 2, 3)), pick(rx, (5, 2, 3, 4))),
        jnp.where(low, pick(rx, (0, 3, 2, 1)), pick(rx, (5, 4, 3, 2))),
        jnp.where(low, pick(rx, (0, 3, 4, 3)), pick(rx, (1, 2, 3, 2))),
    )
    ups = (
        (low & (rx < 3)) | (~low & (rx > 1)),
        None,
        ~low & (rx < 2),
    )
    downs = (
        None,
        (low & (rx != 1)) | (~low & (rx > 0)),
        ~low & (rx == 0),
    )
    sides = (
        low & ((rx == 1) | (rx == 2)),
        low & (rx == 3),
        (low & (rx == 0)) | (~low & (rx > 0)),
    )

    def hop(piece, way, device):
        ref = landed(piece)
        return remote(ref, ref, bc_send.at[way, piece], bc_recv.at[piece], device)

    def branches(tree):
        return (
            (0, ups[tree], x_up),
            (1, downs[tree], x_down),
            (2, sides[tree], y_side),
            (3, None if tree < 0 else jnp.bool_(True), partner),
        )

    @pl.when(lead)
    def _():
        def beat(tick, carry):
            for tree, (first, number) in enumerate(TREES):
                q = tick - LAG * depths[tree]

                @pl.when((q >= 0) & (q < number))
                def _(tree=tree, first=first, q=q):
                    piece = first + q

                    @pl.when(is_root)
                    def _():
                        stage(piece).wait()

                    @pl.when(jnp.logical_not(is_root))
                    def _():
                        hop(piece, 3, partner).wait_recv()

                    for way, condition, device in branches(tree):
                        if condition is None:
                            continue

                        @pl.when(condition)
                        def _(way=way, device=device):
                            hop(piece, way, device).start()

            return carry

        lax.fori_loop(0, LONGEST + LAG * DEEPEST, beat, 0)

        def settle(q, carry):
            for tree, (first, number) in enumerate(TREES):

                @pl.when(q < number)
                def _(tree=tree, first=first):
                    for way, condition, device in branches(tree):
                        if condition is None:
                            continue

                        @pl.when(condition)
                        def _(way=way, device=device):
                            hop(first + q, way, device).wait_send()

            return carry

        lax.fori_loop(0, LONGEST, settle, 0)

    @pl.when(jnp.logical_not(lead))
    def _():
        def arrive(piece, carry):
            hop(piece, 3, partner).wait_recv()
            return carry

        lax.fori_loop(0, pieces, arrive, 0)

    count = bcnt[0]

    def before(ids, k):
        found = jnp.int32(16)
        for other in range(k):
            found = jnp.where(ids[other] == ids[k], jnp.int32(other), found)
        return found

    def final(ids, target):
        found = jnp.int32(16)
        for other in range(16):
            hit = (ids[other] == target) & (jnp.int32(other) < count)
            found = jnp.where(hit, jnp.int32(other), found)
        return found

    for k in range(16):
        product = jnp.dot(vals[k], xv[bcol[k]], preferred_element_type=F32)
        slots[k] = product + slots[before(brow, k)] if k else product
    for s in range(16):
        value = slots[final(brow, s)].astype(BF16)
        for h in range(PARTS):
            part[h, s] = value[:, h * WIDE : (h + 1) * WIDE]

    def block(new_z, rel):
        return rem(yhi + rel, 2) * 8 + rem(new_z + 8, 8)

    ways = ((0, 1, z_up), (1, -1, z_down))

    def z_first(h, way, sign, device):
        return remote(
            part.at[h, block(z + 4, way)],
            zr.at[way, 0, h, way],
            z_send.at[way, 0, h],
            z_recv.at[way, 0, h],
            device,
        )

    def z_hop(h, way, step, device):
        return remote(
            zs.at[way, step, h],
            zr.at[way, step, h],
            z_send.at[way, step, h],
            z_recv.at[way, step, h],
            device,
        )

    for h in range(PARTS):
        for way, sign, device in ways:
            z_first(h, way, sign, device).start()
    for step in range(1, 4):
        for h in range(PARTS):
            for way, sign, device in ways:
                if step == 1:
                    z_first(h, way, sign, device).wait_recv()
                else:
                    z_hop(h, way, step - 1, device).wait_recv()
                for rel in range(2):
                    value = part[h, block(z + sign * (4 - step), rel)]
                    if step > 1 or rel == way:
                        value = (
                            value.astype(F32) + zr[way, step - 1, h, rel].astype(F32)
                        ).astype(BF16)
                    zs[way, step, h, rel] = value
                z_hop(h, way, step, device).start()

    def y_hop(h):
        return remote(ys.at[h], yr.at[h], y_send.at[h], y_recv.at[h], y_far)

    for h in range(PARTS):
        for way, sign, device in ways:
            z_hop(h, way, 3, device).wait_recv()
        sums = [
            part[h, block(z, rel)].astype(F32)
            + zr[0, 3, h, rel].astype(F32)
            + zr[1, 3, h, rel].astype(F32)
            for rel in range(2)
        ]
        ys[h] = sums[1].astype(BF16)
        y_hop(h).start()
        keep[:, h * WIDE : (h + 1) * WIDE] = sums[0]
    for h in range(PARTS):
        y_hop(h).wait_recv()
    agg = jnp.concatenate(
        [
            (keep[:, h * WIDE : (h + 1) * WIDE] + yr[h].astype(F32)).astype(BF16)
            for h in range(PARTS)
        ],
        axis=1,
    )

    preact = jnp.dot(agg, weight[...], preferred_element_type=F32)
    sigma = jax.nn.sigmoid(preact)
    active = preact * sigma
    out[...] = active.astype(BF16)
    label_line = jnp.broadcast_to(labels[pl.ds(team, 1), :], (128, 128))
    classes = lax.broadcasted_iota(jnp.int32, (128, 128), 0)
    onehot = (label_line == classes).astype(F32).T
    spare = jnp.zeros((120, 512), F32)
    wide_table = jnp.concatenate([table[...].astype(F32), spare], axis=0)
    target = jnp.dot(onehot, wide_table, preferred_element_type=F32)
    known = jnp.broadcast_to(mask[pl.ds(team, 1), :], (128, 128)).astype(F32).T
    known = jnp.concatenate([known] * 4, axis=1)
    residual = known * (active - target)
    slope = sigma * (1.0 + preact * (1.0 - sigma))
    grad_pre = (residual * slope).astype(BF16)
    back = lax.dot_general(
        grad_pre, weight[...], (((1,), (1,)), ((), ())), preferred_element_type=F32
    ).astype(BF16)
    gath[team] = back

    def cols(h):
        return pl.ds(h * AG_WIDE, AG_WIDE)

    def ag_hop(step, way, rel, h, device):
        sign = 1 if way == 0 else -1
        origin = block(z - sign * (step - 1), rel)
        ref = gath.at[origin, :, cols(h)]
        return remote(
            ref, ref, ag_send.at[way, step, rel, h], ag_recv.at[way, step, rel, h], device
        )

    def ag_wait(step, way, rel, h, device):
        sign = 1 if way == 0 else -1
        origin = block(z - sign * step, rel)
        ref = gath.at[origin, :, cols(h)]
        remote(
            ref, ref, ag_send.at[way, step, rel, h], ag_recv.at[way, step, rel, h], device
        ).wait_recv()

    def ag_side(h, slot):
        ref = gath.at[slot, :, cols(h)]
        return remote(ref, ref, y_send.at[PARTS + h], y_recv.at[PARTS + h], y_far)

    for h in range(AG_PARTS):
        ag_side(h, team).start()
        for way, sign, device in ways:
            ag_hop(1, way, 0, h, device).start()
    gw = lax.dot_general(
        agg, grad_pre, (((0,), (0,)), ((), ())), preferred_element_type=F32
    ).reshape(16, 32, 512)
    gw32[...] = gw
    gwb[...] = gw.astype(BF16)

    def peer_row(d):
        return (rem(row + d, 16), team)

    def peer_team(d):
        return (row, rem(team + d, 16))

    def gw_hop(stage_id, d, receive):
        slot_row = rem(row - d + 16, 16) if receive else row
        slot_team = rem(team - d + 16, 16) if receive else team
        to_row, to_team = rem(row + d, 16), rem(team + d, 16)
        if stage_id == 0:
            src, dst, device = gwb.at[to_row], g1r.at[slot_row], peer_row(d)
        elif stage_id == 1:
            src, dst, device = g1t.at[to_team], g2r.at[slot_team], peer_team(d)
        elif stage_id == 2:
            src, dst, device = g3.at[slot_team], g3.at[slot_team], peer_team(d)
        else:
            src, dst, device = g4.at[slot_row], g4.at[slot_row], peer_row(d)
        return remote(
            src, dst, gw_send.at[stage_id, d], gw_recv.at[stage_id, d], device
        )

    def gw_start(stage_id):
        def one(d, carry):
            gw_hop(stage_id, d, False).start()
            return carry

        lax.fori_loop(1, 16, one, 0)

    def gw_arrive(stage_id):
        def one(d, carry):
            gw_hop(stage_id, d, True).wait_recv()
            return carry

        lax.fori_loop(1, 16, one, 0)

    def gw_stage(stage_id):
        gw_arrive(stage_id)
        if stage_id == 0:

            def one(d, total):
                return total + g1r[rem(row + d, 16)].astype(F32)

            total = lax.fori_loop(1, 16, one, gw32[row])
            for a in range(4):
                for b in range(4):
                    g1t[a * 4 + b] = total[a * 8 : a * 8 + 8, b * 128 : b * 128 + 128]
        elif stage_id == 1:

            def one(d, total):
                return total + g2r[rem(team + d, 16)]

            g3[team] = lax.fori_loop(1, 16, one, g1t[team])
        elif stage_id == 2:
            lines = [
                jnp.concatenate([g3[a * 4 + b] for b in range(4)], axis=1)
                for a in range(4)
            ]
            scale = 1.0 / math.sqrt(32768)
            g4[row] = (jnp.concatenate(lines, axis=0) * scale).astype(BF16)
        if stage_id < 3:
            gw_start(stage_id + 1)

    gw_start(0)
    for h in range(AG_PARTS):
        ag_side(h, rem(team + 8, 16)).wait_recv()
        for way, sign, device in ways:
            ag_hop(1, way, 1, h, device).start()
    for step in range(2, 5):
        for rel in range(2):
            for h in range(AG_PARTS):
                for way, sign, device in ways:
                    ag_wait(step - 1, way, rel, h, device)
                    if step < 4 or rel == way:
                        ag_hop(step, way, rel, h, device).start()
        gw_stage(step - 2)
    for rel in range(2):
        for h in range(AG_PARTS):
            ag_wait(4, rel, rel, h, ways[rel][2])

    for k in range(16):
        product = jnp.dot(vt[k], gath[brow[k]], preferred_element_type=F32)
        slots[k] = product + slots[before(bcol, k)] if k else product
    for s in range(16):
        value = slots[final(bcol, s)].astype(BF16)
        for h in range(PARTS):
            sp[h, s % 2, s // 2] = value[:, h * WIDE : (h + 1) * WIDE]

    def p_hop(h):
        return remote(sp.at[h, 1 - core], prx.at[h], p_send.at[h], p_recv.at[h], partner)

    def chip_block(new_x, rel):
        return rem(ylo + rel, 2) * 4 + rem(new_x + 4, 4)

    x_ways = ((0, 1, x_up), (1, -1, x_down))

    def x_first(h, way, device):
        return remote(
            chip.at[h, chip_block(x + 2, way)],
            xr.at[way, 0, h, way],
            x_send.at[way, 0, h],
            x_recv.at[way, 0, h],
            device,
        )

    def x_hop(h, way, device):
        return remote(
            xs.at[way, h],
            xr.at[way, 1, h],
            x_send.at[way, 1, h],
            x_recv.at[way, 1, h],
            device,
        )

    def b_hop(h):
        return remote(bs.at[h], br.at[h], b_send.at[h], b_recv.at[h], y_side)

    for h in range(PARTS):
        p_hop(h).start()
    for h in range(PARTS):
        p_hop(h).wait_recv()

        def fold(m, carry, h=h):
            chip[h, m] = (sp[h, core, m].astype(F32) + prx[h, m].astype(F32)).astype(BF16)
            return carry

        lax.fori_loop(0, 8, fold, 0)
        for way, sign, device in x_ways:
            x_first(h, way, device).start()
    for h in range(PARTS):
        for way, sign, device in x_ways:
            x_first(h, way, device).wait_recv()
            for rel in range(2):
                value = chip[h, chip_block(x + sign, rel)]
                if rel == way:
                    value = (value.astype(F32) + xr[way, 0, h, rel].astype(F32)).astype(BF16)
                xs[way, h, rel] = value
            x_hop(h, way, device).start()
    for h in range(PARTS):
        for way, sign, device in x_ways:
            x_hop(h, way, device).wait_recv()
        sums = [
            chip[h, chip_block(x, rel)].astype(F32)
            + xr[0, 1, h, rel].astype(F32)
            + xr[1, 1, h, rel].astype(F32)
            for rel in range(2)
        ]
        bs[h] = sums[1].astype(BF16)
        b_hop(h).start()
        keep[:, h * WIDE : (h + 1) * WIDE] = sums[0]
    gw_stage(3)
    gw_out[...] = g4[...]
    for h in range(PARTS):
        b_hop(h).wait_recv()
        gf_out[:, h * WIDE : (h + 1) * WIDE] = (
            keep[:, h * WIDE : (h + 1) * WIDE] + br[h].astype(F32)
        ).astype(BF16)

    for h in range(PARTS):
        for way, sign, device in ways:
            z_first(h, way, sign, device).wait_send()
            for step in range(1, 4):
                z_hop(h, way, step, device).wait_send()
        y_hop(h).wait_send()
        p_hop(h).wait_send()
        b_hop(h).wait_send()
        for way, sign, device in x_ways:
            x_first(h, way, device).wait_send()
            x_hop(h, way, device).wait_send()
    for h in range(AG_PARTS):
        ag_side(h, team).wait_send()
        for way, sign, device in ways:
            for rel in range(2):
                for step in range(1, 5):
                    if step < 4 or rel == way:
                        ag_hop(step, way, rel, h, device).wait_send()

    def sent(d, carry):
        for stage_id in range(4):
            gw_hop(stage_id, d, False).wait_send()
        return carry

    lax.fori_loop(1, 16, sent, 0)


def per_device(
    features, weight, table, labels, label_mask, block_vals, block_row, block_col, block_count
):
    vmem = pl.BlockSpec(memory_space=pltpu.VMEM)
    smem = pl.BlockSpec(memory_space=pltpu.SMEM)
    dma = pltpu.SemaphoreType.DMA
    half = (PARTS, 128, WIDE)
    outs = pl.pallas_call(
        layer_kernel,
        out_shape=(
            jax.ShapeDtypeStruct((128, 512), BF16),
            jax.ShapeDtypeStruct((16, 32, 512), BF16),
            jax.ShapeDtypeStruct((128, 512), BF16),
        ),
        in_specs=[pl.BlockSpec(memory_space=pl.ANY)] + [vmem] * 5 + [smem] * 3,
        out_specs=(vmem, vmem, vmem),
        scratch_shapes=[
            pltpu.VMEM((16, 128, 512), BF16),
            pltpu.VMEM((16, 128, 128), BF16),
            pltpu.VMEM((17, 128, 512), F32),
            pltpu.VMEM((PARTS, 16, 128, WIDE), BF16),
            pltpu.VMEM((2, 4, PARTS, 2, 128, WIDE), BF16),
            pltpu.VMEM((2, 4, PARTS, 2, 128, WIDE), BF16),
            pltpu.VMEM(half, BF16),
            pltpu.VMEM(half, BF16),
            pltpu.VMEM((128, 512), F32),
            pltpu.VMEM((16, 128, 512), BF16),
            pltpu.VMEM((16, 32, 512), F32),
            pltpu.VMEM((16, 32, 512), BF16),
            pltpu.VMEM((16, 32, 512), BF16),
            pltpu.VMEM((16, 8, 128), F32),
            pltpu.VMEM((16, 8, 128), F32),
            pltpu.VMEM((16, 8, 128), F32),
            pltpu.VMEM((16, 32, 512), BF16),
            pltpu.VMEM((PARTS, 2, 8, 128, WIDE), BF16),
            pltpu.VMEM((PARTS, 8, 128, WIDE), BF16),
            pltpu.VMEM((PARTS, 8, 128, WIDE), BF16),
            pltpu.VMEM((2, PARTS, 2, 128, WIDE), BF16),
            pltpu.VMEM((2, 2, PARTS, 2, 128, WIDE), BF16),
            pltpu.VMEM(half, BF16),
            pltpu.VMEM(half, BF16),
            dma((64,)),
            dma((4, 64)),
            dma((2, 4, PARTS)),
            dma((2, 4, PARTS)),
            dma((PARTS + AG_PARTS,)),
            dma((PARTS + AG_PARTS,)),
            dma((2, 5, 2, AG_PARTS)),
            dma((2, 5, 2, AG_PARTS)),
            dma((4, 16)),
            dma((4, 16)),
            dma((PARTS,)),
            dma((PARTS,)),
            dma((2, 2, PARTS)),
            dma((2, 2, PARTS)),
            dma((PARTS,)),
            dma((PARTS,)),
        ],
        compiler_params=pltpu.CompilerParams(collective_id=0, has_side_effects=True),
        name="layer",
    )(
        features,
        weight,
        table,
        labels.reshape(16, 128),
        label_mask.reshape(16, 128),
        block_vals[0, 0],
        block_row[0, 0],
        block_col[0, 0],
        block_count[0],
    )
    output, grad_weight, grad_piece = outs
    return (output, grad_weight.reshape(512, 512).astype(F32), grad_piece[None])


def solution(mesh):
    placed = (
        P("row", None),
        P(),
        P(),
        P("row"),
        P("row"),
        P("row", "team", None, None, None),
        P("row", "team", None),
        P("row", "team", None),
        P("row", "team"),
    )
    return jax.shard_map(
        per_device,
        mesh=mesh,
        in_specs=placed,
        out_specs=(P(("row", "team"), None), P(), P("team", "row", None)),
        check_vma=False,
    )
```

```python
import functools
import math

import jax
import jax.numpy as jnp
from jax import lax
from jax.experimental import pallas as pl
from jax.experimental.pallas import tpu as pltpu
from jax.sharding import PartitionSpec as P

MESH = pl.DeviceIdType.MESH
BF16 = jnp.bfloat16
F32 = jnp.float32
PARTS = 4
WIDE = 128
AG_PARTS = 2
AG_WIDE = 256
PIECE = 32
TREES = ((0, 22), (22, 20), (42, 22))
LONGEST = 22
DEEPEST = 4
FED = 42
LAG = 9


def rem(value, size):
    return lax.rem(value, jnp.int32(size))


def div(value, size):
    return lax.div(value, jnp.int32(size))


def remote(src, dst, send_sem, recv_sem, device):
    return pltpu.make_async_remote_copy(
        src_ref=src,
        dst_ref=dst,
        send_sem=send_sem,
        recv_sem=recv_sem,
        device_id=device,
        device_id_type=MESH,
    )


def pick(index, table):
    value = jnp.int32(table[0])
    for position, entry in enumerate(table[1:], 1):
        value = jnp.where(index == position, jnp.int32(entry), value)
    return value


def layer_kernel(
    feat,
    weight,
    table,
    labels,
    mask,
    vals,
    brow,
    bcol,
    bcnt,
    out,
    gw_out,
    gf_out,
    xv,
    vt,
    slots,
    part,
    zs,
    zr,
    ys,
    yr,
    keep,
    gath,
    gw32,
    gwb,
    g1r,
    g1t,
    g2r,
    g3,
    g4,
    sp,
    prx,
    chip,
    xs,
    xr,
    bs,
    br,
    bc_recv,
    bc_send,
    feed_send,
    z_send,
    z_recv,
    y_send,
    y_recv,
    ag_send,
    ag_recv,
    gw_send,
    gw_recv,
    p_send,
    p_recv,
    x_send,
    x_recv,
    b_send,
    b_recv,
):
    row = lax.axis_index("row")
    team = lax.axis_index("team")
    core = rem(row, 2)
    x = rem(div(row, 2), 4)
    ylo = div(row, 8)
    z = rem(team, 8)
    yhi = div(team, 8)

    def at_row(new_y, new_x, new_core):
        return ((new_y * 4 + rem(new_x + 4, 4)) * 2 + new_core, team)

    def at_team(new_yhi, new_z):
        return (row, new_yhi * 8 + rem(new_z + 8, 8))

    partner = at_row(ylo, x, 1 - core)
    x_up, x_down = at_row(ylo, x + 1, core), at_row(ylo, x - 1, core)
    y_side = at_row(1 - ylo, x, core)
    z_up, z_down = at_team(yhi, z + 1), at_team(yhi, z - 1)
    y_far = at_team(1 - yhi, z)

    barrier = pltpu.get_barrier_semaphore()

    def greet(d, carry):
        pl.semaphore_signal(
            barrier, inc=1, device_id=(rem(row + d, 16), team), device_id_type=MESH
        )
        pl.semaphore_signal(
            barrier, inc=1, device_id=(row, rem(team + d, 16)), device_id_type=MESH
        )
        return carry

    lax.fori_loop(1, 16, greet, 0)
    fed = (((1 - ylo) * 4 + x) * 2 + core, rem(team + 8, 16))
    pl.semaphore_signal(barrier, inc=1, device_id=fed, device_id_type=MESH)

    root = team
    root_core = rem(root, 2)
    rx = rem(x - rem(div(root, 2), 4) + 4, 4)
    ry = rem(ylo + div(root, 8), 2)
    lead = core == root_core
    is_root = row == root
    pieces = feat.shape[0] // PIECE

    def landed(piece):
        return xv.at[
            div(piece, 128 // PIECE),
            pl.ds(pl.multiple_of(rem(piece, 128 // PIECE) * PIECE, PIECE), PIECE),
        ]

    def stage(piece):
        return pltpu.make_async_copy(
            feat.at[pl.ds(pl.multiple_of(piece * PIECE, PIECE), PIECE)],
            landed(piece),
            bc_recv.at[piece],
        )

    @pl.when(is_root)
    def _():
        def begin(piece, carry):
            stage(piece).start()
            return carry

        lax.fori_loop(0, pieces, begin, 0)

    slots[16] = jnp.zeros((128, 512), F32)
    for k in range(16):
        vt[k] = vals[k].T

    pl.semaphore_wait(barrier, 31)

    feeder = row == rem(team + 8, 16)

    def feed(piece):
        return remote(
            feat.at[pl.ds(pl.multiple_of(piece * PIECE, PIECE), PIECE)],
            landed(piece),
            feed_send.at[piece],
            bc_recv.at[piece],
            fed,
        )

    @pl.when(feeder)
    def _():
        def begin(q, carry):
            feed(q).start()

            @pl.when(q < TREES[1][1])
            def _():
                feed(TREES[1][0] + q).start()

            return carry

        lax.fori_loop(0, LONGEST, begin, 0)

    low = ry == 0
    depths = (
        jnp.where(low, pick(rx, (0, 1, 2, 3)), pick(rx, (3, 2, 3, 4))),
        jnp.where(low, pick(rx, (0, 3, 2, 1)), pick(rx, (3, 4, 3, 2))),
        jnp.where(low, pick(rx, (0, 3, 4, 3)), pick(rx, (1, 2, 3, 2))),
    )
    ups = (
        (low & (rx < 3)) | (~low & (rx == 2)),
        None,
        ~low & (rx < 2),
    )
    downs = (
        None,
        (low & (rx != 1)) | (~low & (rx > 1)),
        ~low & (rx == 0),
    )
    sides = (
        low & ((rx == 1) | (rx == 2)),
        low & (rx == 3),
        (low & (rx == 0)) | (~low & (rx > 0)),
    )

    def hop(piece, way, device):
        ref = landed(piece)
        return remote(ref, ref, bc_send.at[way, piece], bc_recv.at[piece], device)

    def branches(tree):
        return (
            (0, ups[tree], x_up),
            (1, downs[tree], x_down),
            (2, sides[tree], y_side),
            (3, None if tree < 0 else jnp.bool_(True), partner),
        )

    @pl.when(lead)
    def _():
        def beat(tick, carry):
            for tree, (first, number) in enumerate(TREES):
                q = tick - LAG * depths[tree]

                @pl.when((q >= 0) & (q < number))
                def _(tree=tree, first=first, q=q):
                    piece = first + q

                    @pl.when(is_root)
                    def _():
                        stage(piece).wait()

                    @pl.when(jnp.logical_not(is_root))
                    def _():
                        hop(piece, 3, partner).wait_recv()

                    for way, condition, device in branches(tree):
                        if condition is None:
                            continue

                        @pl.when(condition)
                        def _(way=way, device=device):
                            hop(piece, way, device).start()

            return carry

        lax.fori_loop(0, LONGEST + LAG * DEEPEST, beat, 0)

    @pl.when(jnp.logical_not(lead))
    def _():
        def arrive(piece, carry):
            hop(piece, 3, partner).wait_recv()
            return carry

        lax.fori_loop(0, pieces, arrive, 0)

    count = bcnt[0]

    def before(ids, k):
        found = jnp.int32(16)
        for other in range(k):
            found = jnp.where(ids[other] == ids[k], jnp.int32(other), found)
        return found

    def final(ids, target):
        found = jnp.int32(16)
        for other in range(16):
            hit = (ids[other] == target) & (jnp.int32(other) < count)
            found = jnp.where(hit, jnp.int32(other), found)
        return found

    for k in range(16):
        product = jnp.dot(vals[k], xv[bcol[k]], preferred_element_type=F32)
        slots[k] = product + slots[before(brow, k)] if k else product
    for s in range(16):
        value = slots[final(brow, s)].astype(BF16)
        for h in range(PARTS):
            part[h, s] = value[:, h * WIDE : (h + 1) * WIDE]

    def block(new_z, rel):
        return rem(yhi + rel, 2) * 8 + rem(new_z + 8, 8)

    ways = ((0, 1, z_up), (1, -1, z_down))

    def z_first(h, way, sign, device):
        return remote(
            part.at[h, block(z + 4, way)],
            zr.at[way, 0, h, way],
            z_send.at[way, 0, h],
            z_recv.at[way, 0, h],
            device,
        )

    def z_hop(h, way, step, device):
        return remote(
            zs.at[way, step, h],
            zr.at[way, step, h],
            z_send.at[way, step, h],
            z_recv.at[way, step, h],
            device,
        )

    for h in range(PARTS):
        for way, sign, device in ways:
            z_first(h, way, sign, device).start()

    @pl.when(lead)
    def _():
        def settle(q, carry):
            for tree, (first, number) in enumerate(TREES):

                @pl.when(q < number)
                def _(tree=tree, first=first):
                    for way, condition, device in branches(tree):
                        if condition is None:
                            continue

                        @pl.when(condition)
                        def _(way=way, device=device):
                            hop(first + q, way, device).wait_send()

            return carry

        lax.fori_loop(0, LONGEST, settle, 0)

    @pl.when(feeder)
    def _():
        def fed_all(piece, carry):
            feed(piece).wait_send()
            return carry

        lax.fori_loop(0, FED, fed_all, 0)

    for step in range(1, 4):
        for h in range(PARTS):
            for way, sign, device in ways:
                if step == 1:
                    z_first(h, way, sign, device).wait_recv()
                else:
                    z_hop(h, way, step - 1, device).wait_recv()
                for rel in range(2):
                    value = part[h, block(z + sign * (4 - step), rel)]
                    if step > 1 or rel == way:
                        value = (
                            value.astype(F32) + zr[way, step - 1, h, rel].astype(F32)
                        ).astype(BF16)
                    zs[way, step, h, rel] = value
                z_hop(h, way, step, device).start()

    def y_hop(h):
        return remote(ys.at[h], yr.at[h], y_send.at[h], y_recv.at[h], y_far)

    for h in range(PARTS):
        for way, sign, device in ways:
            z_hop(h, way, 3, device).wait_recv()
        sums = [
            part[h, block(z, rel)].astype(F32)
            + zr[0, 3, h, rel].astype(F32)
            + zr[1, 3, h, rel].astype(F32)
            for rel in range(2)
        ]
        ys[h] = sums[1].astype(BF16)
        y_hop(h).start()
        keep[:, h * WIDE : (h + 1) * WIDE] = sums[0]
    for h in range(PARTS):
        y_hop(h).wait_recv()
    agg = jnp.concatenate(
        [
            (keep[:, h * WIDE : (h + 1) * WIDE] + yr[h].astype(F32)).astype(BF16)
            for h in range(PARTS)
        ],
        axis=1,
    )

    preact = jnp.dot(agg, weight[...], preferred_element_type=F32)
    sigma = jax.nn.sigmoid(preact)
    active = preact * sigma
    out[...] = active.astype(BF16)
    label_line = jnp.broadcast_to(labels[pl.ds(team, 1), :], (128, 128))
    classes = lax.broadcasted_iota(jnp.int32, (128, 128), 0)
    onehot = (label_line == classes).astype(F32).T
    spare = jnp.zeros((120, 512), F32)
    wide_table = jnp.concatenate([table[...].astype(F32), spare], axis=0)
    target = jnp.dot(onehot, wide_table, preferred_element_type=F32)
    known = jnp.broadcast_to(mask[pl.ds(team, 1), :], (128, 128)).astype(F32).T
    known = jnp.concatenate([known] * 4, axis=1)
    residual = known * (active - target)
    slope = sigma * (1.0 + preact * (1.0 - sigma))
    grad_pre = (residual * slope).astype(BF16)
    back = lax.dot_general(
        grad_pre, weight[...], (((1,), (1,)), ((), ())), preferred_element_type=F32
    ).astype(BF16)
    gath[team] = back

    def cols(h):
        return pl.ds(h * AG_WIDE, AG_WIDE)

    def ag_hop(step, way, rel, h, device):
        sign = 1 if way == 0 else -1
        origin = block(z - sign * (step - 1), rel)
        ref = gath.at[origin, :, cols(h)]
        return remote(
            ref, ref, ag_send.at[way, step, rel, h], ag_recv.at[way, step, rel, h], device
        )

    def ag_wait(step, way, rel, h, device):
        sign = 1 if way == 0 else -1
        origin = block(z - sign * step, rel)
        ref = gath.at[origin, :, cols(h)]
        remote(
            ref, ref, ag_send.at[way, step, rel, h], ag_recv.at[way, step, rel, h], device
        ).wait_recv()

    def ag_side(h, slot):
        ref = gath.at[slot, :, cols(h)]
        return remote(ref, ref, y_send.at[PARTS + h], y_recv.at[PARTS + h], y_far)

    for h in range(AG_PARTS):
        ag_side(h, team).start()
        for way, sign, device in ways:
            ag_hop(1, way, 0, h, device).start()
    gw = lax.dot_general(
        agg, grad_pre, (((0,), (0,)), ((), ())), preferred_element_type=F32
    ).reshape(16, 32, 512)
    gw32[...] = gw
    gwb[...] = gw.astype(BF16)

    def peer_row(d):
        return (rem(row + d, 16), team)

    def peer_team(d):
        return (row, rem(team + d, 16))

    def gw_hop(stage_id, d, receive):
        slot_row = rem(row - d + 16, 16) if receive else row
        slot_team = rem(team - d + 16, 16) if receive else team
        to_row, to_team = rem(row + d, 16), rem(team + d, 16)
        if stage_id == 0:
            src, dst, device = gwb.at[to_row], g1r.at[slot_row], peer_row(d)
        elif stage_id == 1:
            src, dst, device = g1t.at[to_team], g2r.at[slot_team], peer_team(d)
        elif stage_id == 2:
            src, dst, device = g3.at[slot_team], g3.at[slot_team], peer_team(d)
        else:
            spot = g4.at[div(slot_row, 2), rem(slot_row, 2)]
            src, dst, device = spot, spot, peer_row(d)
        return remote(
            src, dst, gw_send.at[stage_id, d], gw_recv.at[stage_id, d], device
        )

    def gw_start(stage_id):
        def one(d, carry):
            gw_hop(stage_id, d, False).start()
            return carry

        lax.fori_loop(1, 16, one, 0)

    def gw_arrive(stage_id):
        def one(d, carry):
            gw_hop(stage_id, d, True).wait_recv()
            return carry

        lax.fori_loop(1, 16, one, 0)

    def gw_stage(stage_id):
        gw_arrive(stage_id)
        if stage_id == 0:

            def one(d, total):
                return total + g1r[rem(row + d, 16)].astype(F32)

            total = lax.fori_loop(1, 16, one, gw32[row])
            for a in range(4):
                for b in range(4):
                    g1t[a * 4 + b] = total[a * 8 : a * 8 + 8, b * 128 : b * 128 + 128]
        elif stage_id == 1:

            def one(d, total):
                return total + g2r[rem(team + d, 16)]

            g3[team] = lax.fori_loop(1, 16, one, g1t[team])
        elif stage_id == 2:
            lines = [
                jnp.concatenate([g3[a * 4 + b] for b in range(4)], axis=1)
                for a in range(4)
            ]
            scale = 1.0 / math.sqrt(32768)
            g4[div(row, 2), core] = (jnp.concatenate(lines, axis=0) * scale).astype(BF16)
        if stage_id < 2:
            gw_start(stage_id + 1)
        else:
            for d in range(2, 16, 2):
                gw_hop(3, d, False).start()

    def gw_across(receive):
        side = g4.at[:, 1 - core if receive else core]
        return remote(side, side, gw_send.at[3, 1], gw_recv.at[3, 1], partner)

    gw_start(0)
    for h in range(PARTS):
        for way, sign, device in ways:
            z_first(h, way, sign, device).wait_send()
            for step in range(1, 4):
                z_hop(h, way, step, device).wait_send()
        y_hop(h).wait_send()
    for h in range(AG_PARTS):
        ag_side(h, rem(team + 8, 16)).wait_recv()
        for way, sign, device in ways:
            ag_hop(1, way, 1, h, device).start()
    for step in range(2, 5):
        for rel in range(2):
            for h in range(AG_PARTS):
                for way, sign, device in ways:
                    ag_wait(step - 1, way, rel, h, device)
                    if step < 4 or rel == way:
                        ag_hop(step, way, rel, h, device).start()
        if step == 3:
            gw_stage(0)
    for rel in range(2):
        for h in range(AG_PARTS):
            ag_wait(4, rel, rel, h, ways[rel][2])
    gw_stage(1)

    for k in range(16):
        product = jnp.dot(vt[k], gath[brow[k]], preferred_element_type=F32)
        slots[k] = product + slots[before(bcol, k)] if k else product
    for s in range(16):
        value = slots[final(bcol, s)].astype(BF16)
        for h in range(PARTS):
            sp[h, s % 2, s // 2] = value[:, h * WIDE : (h + 1) * WIDE]

    def p_hop(h):
        return remote(sp.at[h, 1 - core], prx.at[h], p_send.at[h], p_recv.at[h], partner)

    def chip_block(new_x, rel):
        return rem(ylo + rel, 2) * 4 + rem(new_x + 4, 4)

    x_ways = ((0, 1, x_up), (1, -1, x_down))

    def x_first(h, way, device):
        return remote(
            chip.at[h, chip_block(x + 2, way)],
            xr.at[way, 0, h, way],
            x_send.at[way, 0, h],
            x_recv.at[way, 0, h],
            device,
        )

    def x_hop(h, way, device):
        return remote(
            xs.at[way, h],
            xr.at[way, 1, h],
            x_send.at[way, 1, h],
            x_recv.at[way, 1, h],
            device,
        )

    def b_hop(h):
        return remote(bs.at[h], br.at[h], b_send.at[h], b_recv.at[h], y_side)

    for h in range(PARTS):
        p_hop(h).start()
    gw_stage(2)
    for h in range(PARTS):
        p_hop(h).wait_recv()

        def fold(m, carry, h=h):
            chip[h, m] = (sp[h, core, m].astype(F32) + prx[h, m].astype(F32)).astype(BF16)
            return carry

        lax.fori_loop(0, 8, fold, 0)
        for way, sign, device in x_ways:
            x_first(h, way, device).start()
    for h in range(AG_PARTS):
        ag_side(h, team).wait_send()
        for way, sign, device in ways:
            for rel in range(2):
                for step in range(1, 5):
                    if step < 4 or rel == way:
                        ag_hop(step, way, rel, h, device).wait_send()

    def sent(d, carry):
        for stage_id in range(3):
            gw_hop(stage_id, d, False).wait_send()
        return carry

    lax.fori_loop(1, 16, sent, 0)
    for h in range(PARTS):
        for way, sign, device in x_ways:
            x_first(h, way, device).wait_recv()
            for rel in range(2):
                value = chip[h, chip_block(x + sign, rel)]
                if rel == way:
                    value = (value.astype(F32) + xr[way, 0, h, rel].astype(F32)).astype(BF16)
                xs[way, h, rel] = value
            x_hop(h, way, device).start()
    for h in range(PARTS):
        for way, sign, device in x_ways:
            x_hop(h, way, device).wait_recv()
        sums = [
            chip[h, chip_block(x, rel)].astype(F32)
            + xr[0, 1, h, rel].astype(F32)
            + xr[1, 1, h, rel].astype(F32)
            for rel in range(2)
        ]
        bs[h] = sums[1].astype(BF16)
        b_hop(h).start()
        keep[:, h * WIDE : (h + 1) * WIDE] = sums[0]
    for d in range(2, 16, 2):
        gw_hop(3, d, True).wait_recv()
    gw_across(False).start()
    for h in range(PARTS):
        b_hop(h).wait_recv()
        gf_out[:, h * WIDE : (h + 1) * WIDE] = (
            keep[:, h * WIDE : (h + 1) * WIDE] + br[h].astype(F32)
        ).astype(BF16)

    gw_across(True).wait_recv()
    gw_out[...] = g4[...].reshape(16, 32, 512)
    for d in range(2, 16, 2):
        gw_hop(3, d, False).wait_send()
    gw_across(False).wait_send()
    for h in range(PARTS):
        p_hop(h).wait_send()
        b_hop(h).wait_send()
        for way, sign, device in x_ways:
            x_first(h, way, device).wait_send()
            x_hop(h, way, device).wait_send()


def per_device(
    features, weight, table, labels, label_mask, block_vals, block_row, block_col, block_count
):
    vmem = pl.BlockSpec(memory_space=pltpu.VMEM)
    smem = pl.BlockSpec(memory_space=pltpu.SMEM)
    dma = pltpu.SemaphoreType.DMA
    half = (PARTS, 128, WIDE)
    outs = pl.pallas_call(
        layer_kernel,
        out_shape=(
            jax.ShapeDtypeStruct((128, 512), BF16),
            jax.ShapeDtypeStruct((16, 32, 512), BF16),
            jax.ShapeDtypeStruct((128, 512), BF16),
        ),
        in_specs=[pl.BlockSpec(memory_space=pl.ANY)] + [vmem] * 5 + [smem] * 3,
        out_specs=(vmem, vmem, vmem),
        scratch_shapes=[
            pltpu.VMEM((16, 128, 512), BF16),
            pltpu.VMEM((16, 128, 128), BF16),
            pltpu.VMEM((17, 128, 512), F32),
            pltpu.VMEM((PARTS, 16, 128, WIDE), BF16),
            pltpu.VMEM((2, 4, PARTS, 2, 128, WIDE), BF16),
            pltpu.VMEM((2, 4, PARTS, 2, 128, WIDE), BF16),
            pltpu.VMEM(half, BF16),
            pltpu.VMEM(half, BF16),
            pltpu.VMEM((128, 512), F32),
            pltpu.VMEM((16, 128, 512), BF16),
            pltpu.VMEM((16, 32, 512), F32),
            pltpu.VMEM((16, 32, 512), BF16),
            pltpu.VMEM((16, 32, 512), BF16),
            pltpu.VMEM((16, 8, 128), F32),
            pltpu.VMEM((16, 8, 128), F32),
            pltpu.VMEM((16, 8, 128), F32),
            pltpu.VMEM((8, 2, 32, 512), BF16),
            pltpu.VMEM((PARTS, 2, 8, 128, WIDE), BF16),
            pltpu.VMEM((PARTS, 8, 128, WIDE), BF16),
            pltpu.VMEM((PARTS, 8, 128, WIDE), BF16),
            pltpu.VMEM((2, PARTS, 2, 128, WIDE), BF16),
            pltpu.VMEM((2, 2, PARTS, 2, 128, WIDE), BF16),
            pltpu.VMEM(half, BF16),
            pltpu.VMEM(half, BF16),
            dma((64,)),
            dma((4, 64)),
            dma((64,)),
            dma((2, 4, PARTS)),
            dma((2, 4, PARTS)),
            dma((PARTS + AG_PARTS,)),
            dma((PARTS + AG_PARTS,)),
            dma((2, 5, 2, AG_PARTS)),
            dma((2, 5, 2, AG_PARTS)),
            dma((4, 16)),
            dma((4, 16)),
            dma((PARTS,)),
            dma((PARTS,)),
            dma((2, 2, PARTS)),
            dma((2, 2, PARTS)),
            dma((PARTS,)),
            dma((PARTS,)),
        ],
        compiler_params=pltpu.CompilerParams(collective_id=0, has_side_effects=True),
        name="layer",
    )(
        features,
        weight,
        table,
        labels.reshape(16, 128),
        label_mask.reshape(16, 128),
        block_vals[0, 0],
        block_row[0, 0],
        block_col[0, 0],
        block_count[0],
    )
    output, grad_weight, grad_piece = outs
    return (output, grad_weight.reshape(512, 512).astype(F32), grad_piece[None])


def solution(mesh):
    placed = (
        P("row", None),
        P(),
        P(),
        P("row"),
        P("row"),
        P("row", "team", None, None, None),
        P("row", "team", None),
        P("row", "team", None),
        P("row", "team"),
    )
    return jax.shard_map(
        per_device,
        mesh=mesh,
        in_specs=placed,
        out_specs=(P(("row", "team"), None), P(), P("team", "row", None)),
        check_vma=False,
    )
```

```python
import functools
import math

import jax
import jax.numpy as jnp
from jax import lax
from jax.experimental import pallas as pl
from jax.experimental.pallas import tpu as pltpu
from jax.sharding import PartitionSpec as P

MESH = pl.DeviceIdType.MESH
BF16 = jnp.bfloat16
F32 = jnp.float32
PARTS = 4
WIDE = 128
AG_PARTS = 2
AG_WIDE = 256
PIECE = 32
TREES = ((0, 22), (22, 20), (42, 22))
LONGEST = 22
DEEPEST = 4
FED = 42
LAG = 9


def rem(value, size):
    return lax.rem(value, jnp.int32(size))


def div(value, size):
    return lax.div(value, jnp.int32(size))


def remote(src, dst, send_sem, recv_sem, device):
    return pltpu.make_async_remote_copy(
        src_ref=src,
        dst_ref=dst,
        send_sem=send_sem,
        recv_sem=recv_sem,
        device_id=device,
        device_id_type=MESH,
    )


def pick(index, table):
    value = jnp.int32(table[0])
    for position, entry in enumerate(table[1:], 1):
        value = jnp.where(index == position, jnp.int32(entry), value)
    return value


def layer_kernel(
    feat,
    weight,
    table,
    labels,
    mask,
    vals,
    brow,
    bcol,
    bcnt,
    out,
    gw_out,
    gf_out,
    xv,
    vt,
    slots,
    part,
    zs,
    zr,
    ys,
    yr,
    keep,
    gath,
    gw32,
    gwb,
    gcr,
    gc32,
    gcb,
    g1r,
    g1t,
    g2r,
    g3,
    g4,
    sp,
    prx,
    chip,
    xs,
    xr,
    bs,
    br,
    bc_recv,
    bc_send,
    feed_send,
    z_send,
    z_recv,
    y_send,
    y_recv,
    ag_send,
    ag_recv,
    gw_send,
    gw_recv,
    p_send,
    p_recv,
    x_send,
    x_recv,
    b_send,
    b_recv,
):
    row = lax.axis_index("row")
    team = lax.axis_index("team")
    core = rem(row, 2)
    x = rem(div(row, 2), 4)
    ylo = div(row, 8)
    z = rem(team, 8)
    yhi = div(team, 8)

    def at_row(new_y, new_x, new_core):
        return ((new_y * 4 + rem(new_x + 4, 4)) * 2 + new_core, team)

    def at_team(new_yhi, new_z):
        return (row, new_yhi * 8 + rem(new_z + 8, 8))

    partner = at_row(ylo, x, 1 - core)
    x_up, x_down = at_row(ylo, x + 1, core), at_row(ylo, x - 1, core)
    y_side = at_row(1 - ylo, x, core)
    z_up, z_down = at_team(yhi, z + 1), at_team(yhi, z - 1)
    y_far = at_team(1 - yhi, z)

    barrier = pltpu.get_barrier_semaphore()

    def greet(d, carry):
        pl.semaphore_signal(
            barrier, inc=1, device_id=(rem(row + d, 16), team), device_id_type=MESH
        )
        pl.semaphore_signal(
            barrier, inc=1, device_id=(row, rem(team + d, 16)), device_id_type=MESH
        )
        return carry

    lax.fori_loop(1, 16, greet, 0)
    fed = (((1 - ylo) * 4 + x) * 2 + core, rem(team + 8, 16))
    pl.semaphore_signal(barrier, inc=1, device_id=fed, device_id_type=MESH)

    root = team
    root_core = rem(root, 2)
    rx = rem(x - rem(div(root, 2), 4) + 4, 4)
    ry = rem(ylo + div(root, 8), 2)
    lead = core == root_core
    is_root = row == root
    pieces = feat.shape[0] // PIECE

    def landed(piece):
        return xv.at[
            div(piece, 128 // PIECE),
            pl.ds(pl.multiple_of(rem(piece, 128 // PIECE) * PIECE, PIECE), PIECE),
        ]

    def stage(piece):
        return pltpu.make_async_copy(
            feat.at[pl.ds(pl.multiple_of(piece * PIECE, PIECE), PIECE)],
            landed(piece),
            bc_recv.at[piece],
        )

    @pl.when(is_root)
    def _():
        def begin(piece, carry):
            stage(piece).start()
            return carry

        lax.fori_loop(0, pieces, begin, 0)

    slots[16] = jnp.zeros((128, 512), F32)
    for k in range(16):
        vt[k] = vals[k].T

    pl.semaphore_wait(barrier, 31)

    feeder = row == rem(team + 8, 16)

    def feed(piece):
        return remote(
            feat.at[pl.ds(pl.multiple_of(piece * PIECE, PIECE), PIECE)],
            landed(piece),
            feed_send.at[piece],
            bc_recv.at[piece],
            fed,
        )

    @pl.when(feeder)
    def _():
        def begin(q, carry):
            feed(q).start()

            @pl.when(q < TREES[1][1])
            def _():
                feed(TREES[1][0] + q).start()

            return carry

        lax.fori_loop(0, LONGEST, begin, 0)

    low = ry == 0
    depths = (
        jnp.where(low, pick(rx, (0, 1, 2, 3)), pick(rx, (3, 2, 3, 4))),
        jnp.where(low, pick(rx, (0, 3, 2, 1)), pick(rx, (3, 4, 3, 2))),
        jnp.where(low, pick(rx, (0, 3, 4, 3)), pick(rx, (1, 2, 3, 2))),
    )
    ups = (
        (low & (rx < 3)) | (~low & (rx == 2)),
        None,
        ~low & (rx < 2),
    )
    downs = (
        None,
        (low & (rx != 1)) | (~low & (rx > 1)),
        ~low & (rx == 0),
    )
    sides = (
        low & ((rx == 1) | (rx == 2)),
        low & (rx == 3),
        (low & (rx == 0)) | (~low & (rx > 0)),
    )

    def hop(piece, way, device):
        ref = landed(piece)
        return remote(ref, ref, bc_send.at[way, piece], bc_recv.at[piece], device)

    def branches(tree):
        return (
            (0, ups[tree], x_up),
            (1, downs[tree], x_down),
            (2, sides[tree], y_side),
            (3, None if tree < 0 else jnp.bool_(True), partner),
        )

    @pl.when(lead)
    def _():
        def beat(tick, carry):
            for tree, (first, number) in enumerate(TREES):
                q = tick - LAG * depths[tree]

                @pl.when((q >= 0) & (q < number))
                def _(tree=tree, first=first, q=q):
                    piece = first + q

                    @pl.when(is_root)
                    def _():
                        stage(piece).wait()

                    @pl.when(jnp.logical_not(is_root))
                    def _():
                        hop(piece, 3, partner).wait_recv()

                    for way, condition, device in branches(tree):
                        if condition is None:
                            continue

                        @pl.when(condition)
                        def _(way=way, device=device):
                            hop(piece, way, device).start()

            return carry

        lax.fori_loop(0, LONGEST + LAG * DEEPEST, beat, 0)

    @pl.when(jnp.logical_not(lead))
    def _():
        def arrive(piece, carry):
            hop(piece, 3, partner).wait_recv()
            return carry

        lax.fori_loop(0, pieces, arrive, 0)

    count = bcnt[0]

    def before(ids, k):
        found = jnp.int32(16)
        for other in range(k):
            found = jnp.where(ids[other] == ids[k], jnp.int32(other), found)
        return found

    def final(ids, target):
        found = jnp.int32(16)
        for other in range(16):
            hit = (ids[other] == target) & (jnp.int32(other) < count)
            found = jnp.where(hit, jnp.int32(other), found)
        return found

    for k in range(16):
        product = jnp.dot(vals[k], xv[bcol[k]], preferred_element_type=F32)
        slots[k] = product + slots[before(brow, k)] if k else product
    for s in range(16):
        value = slots[final(brow, s)].astype(BF16)
        for h in range(PARTS):
            part[h, s] = value[:, h * WIDE : (h + 1) * WIDE]

    def block(new_z, rel):
        return rem(yhi + rel, 2) * 8 + rem(new_z + 8, 8)

    ways = ((0, 1, z_up), (1, -1, z_down))

    def z_first(h, way, sign, device):
        return remote(
            part.at[h, block(z + 4, way)],
            zr.at[way, 0, h, way],
            z_send.at[way, 0, h],
            z_recv.at[way, 0, h],
            device,
        )

    def z_hop(h, way, step, device):
        return remote(
            zs.at[way, step, h],
            zr.at[way, step, h],
            z_send.at[way, step, h],
            z_recv.at[way, step, h],
            device,
        )

    for h in range(PARTS):
        for way, sign, device in ways:
            z_first(h, way, sign, device).start()

    @pl.when(lead)
    def _():
        def settle(q, carry):
            for tree, (first, number) in enumerate(TREES):

                @pl.when(q < number)
                def _(tree=tree, first=first):
                    for way, condition, device in branches(tree):
                        if condition is None:
                            continue

                        @pl.when(condition)
                        def _(way=way, device=device):
                            hop(first + q, way, device).wait_send()

            return carry

        lax.fori_loop(0, LONGEST, settle, 0)

    @pl.when(feeder)
    def _():
        def fed_all(piece, carry):
            feed(piece).wait_send()
            return carry

        lax.fori_loop(0, FED, fed_all, 0)

    for step in range(1, 4):
        for h in range(PARTS):
            for way, sign, device in ways:
                if step == 1:
                    z_first(h, way, sign, device).wait_recv()
                else:
                    z_hop(h, way, step - 1, device).wait_recv()
                for rel in range(2):
                    value = part[h, block(z + sign * (4 - step), rel)]
                    if step > 1 or rel == way:
                        value = (
                            value.astype(F32) + zr[way, step - 1, h, rel].astype(F32)
                        ).astype(BF16)
                    zs[way, step, h, rel] = value
                z_hop(h, way, step, device).start()

    def y_hop(h):
        return remote(ys.at[h], yr.at[h], y_send.at[h], y_recv.at[h], y_far)

    for h in range(PARTS):
        for way, sign, device in ways:
            z_hop(h, way, 3, device).wait_recv()
        sums = [
            part[h, block(z, rel)].astype(F32)
            + zr[0, 3, h, rel].astype(F32)
            + zr[1, 3, h, rel].astype(F32)
            for rel in range(2)
        ]
        ys[h] = sums[1].astype(BF16)
        y_hop(h).start()
        keep[:, h * WIDE : (h + 1) * WIDE] = sums[0]
    for h in range(PARTS):
        y_hop(h).wait_recv()
    agg = jnp.concatenate(
        [
            (keep[:, h * WIDE : (h + 1) * WIDE] + yr[h].astype(F32)).astype(BF16)
            for h in range(PARTS)
        ],
        axis=1,
    )

    preact = jnp.dot(agg, weight[...], preferred_element_type=F32)
    sigma = jax.nn.sigmoid(preact)
    active = preact * sigma
    out[...] = active.astype(BF16)
    label_line = jnp.broadcast_to(labels[pl.ds(team, 1), :], (128, 128))
    classes = lax.broadcasted_iota(jnp.int32, (128, 128), 0)
    onehot = (label_line == classes).astype(F32).T
    spare = jnp.zeros((120, 512), F32)
    wide_table = jnp.concatenate([table[...].astype(F32), spare], axis=0)
    target = jnp.dot(onehot, wide_table, preferred_element_type=F32)
    known = jnp.broadcast_to(mask[pl.ds(team, 1), :], (128, 128)).astype(F32).T
    known = jnp.concatenate([known] * 4, axis=1)
    residual = known * (active - target)
    slope = sigma * (1.0 + preact * (1.0 - sigma))
    grad_pre = (residual * slope).astype(BF16)
    back = lax.dot_general(
        grad_pre, weight[...], (((1,), (1,)), ((), ())), preferred_element_type=F32
    ).astype(BF16)
    gath[team] = back

    def cols(h):
        return pl.ds(h * AG_WIDE, AG_WIDE)

    def ag_hop(step, way, rel, h, device):
        sign = 1 if way == 0 else -1
        origin = block(z - sign * (step - 1), rel)
        ref = gath.at[origin, :, cols(h)]
        return remote(
            ref, ref, ag_send.at[way, step, rel, h], ag_recv.at[way, step, rel, h], device
        )

    def ag_wait(step, way, rel, h, device):
        sign = 1 if way == 0 else -1
        origin = block(z - sign * step, rel)
        ref = gath.at[origin, :, cols(h)]
        remote(
            ref, ref, ag_send.at[way, step, rel, h], ag_recv.at[way, step, rel, h], device
        ).wait_recv()

    def ag_side(h, slot):
        ref = gath.at[slot, :, cols(h)]
        return remote(ref, ref, y_send.at[PARTS + h], y_recv.at[PARTS + h], y_far)

    def gw_pair():
        return remote(
            gwb.at[:, 1 - core], gcr, gw_send.at[0, 1], gw_recv.at[0, 1], partner
        )

    for h in range(AG_PARTS):
        ag_side(h, team).start()
        for way, sign, device in ways:
            ag_hop(1, way, 0, h, device).start()
    gw = lax.dot_general(
        agg, grad_pre, (((0,), (0,)), ((), ())), preferred_element_type=F32
    ).reshape(8, 2, 32, 512)
    gw32[...] = gw
    gwb[...] = gw.astype(BF16)
    gw_pair().start()

    def peer_row(d):
        return (rem(row + d, 16), team)

    def peer_team(d):
        return (row, rem(team + d, 16))

    def gw_hop(stage_id, d, receive):
        slot_row = rem(row - d + 16, 16) if receive else row
        slot_team = rem(team - d + 16, 16) if receive else team
        to_row, to_team = rem(row + d, 16), rem(team + d, 16)
        if stage_id == 0:
            src, dst, device = gcb.at[div(to_row, 2)], g1r.at[div(slot_row, 2)], peer_row(d)
        elif stage_id == 1:
            src, dst, device = g1t.at[to_team], g2r.at[slot_team], peer_team(d)
        elif stage_id == 2:
            src, dst, device = g3.at[slot_team], g3.at[slot_team], peer_team(d)
        else:
            spot = g4.at[div(slot_row, 2), rem(slot_row, 2)]
            src, dst, device = spot, spot, peer_row(d)
        return remote(
            src, dst, gw_send.at[stage_id, d], gw_recv.at[stage_id, d], device
        )

    def peers(stage_id):
        return range(2, 16, 2) if stage_id in (0, 3) else range(1, 16)

    def gw_start(stage_id):
        for d in peers(stage_id):
            gw_hop(stage_id, d, False).start()

    def gw_arrive(stage_id):
        for d in peers(stage_id):
            gw_hop(stage_id, d, True).wait_recv()

    def gw_chip():
        gw_pair().wait_recv()
        for m in range(8):
            both = gw32[m, core] + gcr[m].astype(F32)
            gc32[m] = both
            gcb[m] = both.astype(BF16)
        gw_start(0)

    def gw_stage(stage_id):
        gw_arrive(stage_id)
        if stage_id == 0:

            total = gc32[div(row, 2)]
            for d in range(1, 8):
                total = total + g1r[rem(div(row, 2) + d, 8)].astype(F32)
            for a in range(4):
                for b in range(4):
                    g1t[a * 4 + b] = total[a * 8 : a * 8 + 8, b * 128 : b * 128 + 128]
        elif stage_id == 1:

            total = g1t[team]
            for d in range(1, 16):
                total = total + g2r[rem(team + d, 16)]
            g3[team] = total
        elif stage_id == 2:
            lines = [
                jnp.concatenate([g3[a * 4 + b] for b in range(4)], axis=1)
                for a in range(4)
            ]
            scale = 1.0 / math.sqrt(32768)
            g4[div(row, 2), core] = (jnp.concatenate(lines, axis=0) * scale).astype(BF16)
        gw_start(stage_id + 1)

    def gw_across(receive):
        side = g4.at[:, 1 - core if receive else core]
        return remote(side, side, gw_send.at[3, 1], gw_recv.at[3, 1], partner)

    for h in range(PARTS):
        for way, sign, device in ways:
            z_first(h, way, sign, device).wait_send()
            for step in range(1, 4):
                z_hop(h, way, step, device).wait_send()
        y_hop(h).wait_send()
    for tick in range(2, 6):
        for rel in range(2):
            step = tick - rel
            if step > 4:
                continue
            for h in range(AG_PARTS):
                if step == 1:
                    ag_side(h, rem(team + 8, 16)).wait_recv()
                for way, sign, device in ways:
                    if step > 1:
                        ag_wait(step - 1, way, rel, h, device)
                    if step < 4 or rel == way:
                        ag_hop(step, way, rel, h, device).start()
        if tick == 2:
            gw_chip()
        elif tick == 4:
            gw_stage(0)
    for rel in range(2):
        for h in range(AG_PARTS):
            ag_wait(4, rel, rel, h, ways[rel][2])
    gw_stage(1)

    for k in range(16):
        product = jnp.dot(vt[k], gath[brow[k]], preferred_element_type=F32)
        slots[k] = product + slots[before(bcol, k)] if k else product
    for s in range(16):
        value = slots[final(bcol, s)].astype(BF16)
        for h in range(PARTS):
            sp[h, s % 2, s // 2] = value[:, h * WIDE : (h + 1) * WIDE]

    def p_hop(h):
        return remote(sp.at[h, 1 - core], prx.at[h], p_send.at[h], p_recv.at[h], partner)

    def chip_block(new_x, rel):
        return rem(ylo + rel, 2) * 4 + rem(new_x + 4, 4)

    x_ways = ((0, 1, x_up), (1, -1, x_down))

    def x_first(h, way, device):
        return remote(
            chip.at[h, chip_block(x + 2, way)],
            xr.at[way, 0, h, way],
            x_send.at[way, 0, h],
            x_recv.at[way, 0, h],
            device,
        )

    def x_hop(h, way, device):
        return remote(
            xs.at[way, h],
            xr.at[way, 1, h],
            x_send.at[way, 1, h],
            x_recv.at[way, 1, h],
            device,
        )

    def b_hop(h):
        return remote(bs.at[h], br.at[h], b_send.at[h], b_recv.at[h], y_side)

    for h in range(PARTS):
        p_hop(h).start()
    gw_stage(2)
    for h in range(PARTS):
        p_hop(h).wait_recv()

        def fold(m, carry, h=h):
            chip[h, m] = (sp[h, core, m].astype(F32) + prx[h, m].astype(F32)).astype(BF16)
            return carry

        lax.fori_loop(0, 8, fold, 0)
        for way, sign, device in x_ways:
            x_first(h, way, device).start()
    for h in range(AG_PARTS):
        ag_side(h, team).wait_send()
        for way, sign, device in ways:
            for rel in range(2):
                for step in range(1, 5):
                    if step < 4 or rel == way:
                        ag_hop(step, way, rel, h, device).wait_send()

    gw_pair().wait_send()
    for stage_id in range(3):
        for d in peers(stage_id):
            gw_hop(stage_id, d, False).wait_send()
    for h in range(PARTS):
        for way, sign, device in x_ways:
            x_first(h, way, device).wait_recv()
            for rel in range(2):
                value = chip[h, chip_block(x + sign, rel)]
                if rel == way:
                    value = (value.astype(F32) + xr[way, 0, h, rel].astype(F32)).astype(BF16)
                xs[way, h, rel] = value
            x_hop(h, way, device).start()
    for h in range(PARTS):
        for way, sign, device in x_ways:
            x_hop(h, way, device).wait_recv()
        sums = [
            chip[h, chip_block(x, rel)].astype(F32)
            + xr[0, 1, h, rel].astype(F32)
            + xr[1, 1, h, rel].astype(F32)
            for rel in range(2)
        ]
        bs[h] = sums[1].astype(BF16)
        b_hop(h).start()
        keep[:, h * WIDE : (h + 1) * WIDE] = sums[0]
    gw_arrive(3)
    gw_across(False).start()
    for h in range(PARTS):
        b_hop(h).wait_recv()
        gf_out[:, h * WIDE : (h + 1) * WIDE] = (
            keep[:, h * WIDE : (h + 1) * WIDE] + br[h].astype(F32)
        ).astype(BF16)

    gw_across(True).wait_recv()
    gw_out[...] = g4[...].reshape(16, 32, 512)
    for d in peers(3):
        gw_hop(3, d, False).wait_send()
    gw_across(False).wait_send()
    for h in range(PARTS):
        p_hop(h).wait_send()
        b_hop(h).wait_send()
        for way, sign, device in x_ways:
            x_first(h, way, device).wait_send()
            x_hop(h, way, device).wait_send()


def per_device(
    features, weight, table, labels, label_mask, block_vals, block_row, block_col, block_count
):
    vmem = pl.BlockSpec(memory_space=pltpu.VMEM)
    smem = pl.BlockSpec(memory_space=pltpu.SMEM)
    dma = pltpu.SemaphoreType.DMA
    half = (PARTS, 128, WIDE)
    outs = pl.pallas_call(
        layer_kernel,
        out_shape=(
            jax.ShapeDtypeStruct((128, 512), BF16),
            jax.ShapeDtypeStruct((16, 32, 512), BF16),
            jax.ShapeDtypeStruct((128, 512), BF16),
        ),
        in_specs=[pl.BlockSpec(memory_space=pl.ANY)] + [vmem] * 5 + [smem] * 3,
        out_specs=(vmem, vmem, vmem),
        scratch_shapes=[
            pltpu.VMEM((16, 128, 512), BF16),
            pltpu.VMEM((16, 128, 128), BF16),
            pltpu.VMEM((17, 128, 512), F32),
            pltpu.VMEM((PARTS, 16, 128, WIDE), BF16),
            pltpu.VMEM((2, 4, PARTS, 2, 128, WIDE), BF16),
            pltpu.VMEM((2, 4, PARTS, 2, 128, WIDE), BF16),
            pltpu.VMEM(half, BF16),
            pltpu.VMEM(half, BF16),
            pltpu.VMEM((128, 512), F32),
            pltpu.VMEM((16, 128, 512), BF16),
            pltpu.VMEM((8, 2, 32, 512), F32),
            pltpu.VMEM((8, 2, 32, 512), BF16),
            pltpu.VMEM((8, 32, 512), BF16),
            pltpu.VMEM((8, 32, 512), F32),
            pltpu.VMEM((8, 32, 512), BF16),
            pltpu.VMEM((8, 32, 512), BF16),
            pltpu.VMEM((16, 8, 128), F32),
            pltpu.VMEM((16, 8, 128), F32),
            pltpu.VMEM((16, 8, 128), F32),
            pltpu.VMEM((8, 2, 32, 512), BF16),
            pltpu.VMEM((PARTS, 2, 8, 128, WIDE), BF16),
            pltpu.VMEM((PARTS, 8, 128, WIDE), BF16),
            pltpu.VMEM((PARTS, 8, 128, WIDE), BF16),
            pltpu.VMEM((2, PARTS, 2, 128, WIDE), BF16),
            pltpu.VMEM((2, 2, PARTS, 2, 128, WIDE), BF16),
            pltpu.VMEM(half, BF16),
            pltpu.VMEM(half, BF16),
            dma((64,)),
            dma((4, 64)),
            dma((64,)),
            dma((2, 4, PARTS)),
            dma((2, 4, PARTS)),
            dma((PARTS + AG_PARTS,)),
            dma((PARTS + AG_PARTS,)),
            dma((2, 5, 2, AG_PARTS)),
            dma((2, 5, 2, AG_PARTS)),
            dma((4, 16)),
            dma((4, 16)),
            dma((PARTS,)),
            dma((PARTS,)),
            dma((2, 2, PARTS)),
            dma((2, 2, PARTS)),
            dma((PARTS,)),
            dma((PARTS,)),
        ],
        compiler_params=pltpu.CompilerParams(collective_id=0, has_side_effects=True),
        name="layer",
    )(
        features,
        weight,
        table,
        labels.reshape(16, 128),
        label_mask.reshape(16, 128),
        block_vals[0, 0],
        block_row[0, 0],
        block_col[0, 0],
        block_count[0],
    )
    output, grad_weight, grad_piece = outs
    return (output, grad_weight.reshape(512, 512).astype(F32), grad_piece[None])


def solution(mesh):
    placed = (
        P("row", None),
        P(),
        P(),
        P("row"),
        P("row"),
        P("row", "team", None, None, None),
        P("row", "team", None),
        P("row", "team", None),
        P("row", "team"),
    )
    return jax.shard_map(
        per_device,
        mesh=mesh,
        in_specs=placed,
        out_specs=(P(("row", "team"), None), P(), P("team", "row", None)),
        check_vma=False,
    )
```

```python
import functools
import math

import jax
import jax.numpy as jnp
from jax import lax
from jax.experimental import pallas as pl
from jax.experimental.pallas import tpu as pltpu
from jax.sharding import PartitionSpec as P

MESH = pl.DeviceIdType.MESH
BF16 = jnp.bfloat16
F32 = jnp.float32
PARTS = 4
WIDE = 128
AG_PARTS = 2
AG_WIDE = 256
PIECE = 32
TREES = ((0, 22), (22, 20), (42, 22))
LONGEST = 22
DEEPEST = 4
FED = 42
LAG = 9


def rem(value, size):
    return lax.rem(value, jnp.int32(size))


def div(value, size):
    return lax.div(value, jnp.int32(size))


def remote(src, dst, send_sem, recv_sem, device):
    return pltpu.make_async_remote_copy(
        src_ref=src,
        dst_ref=dst,
        send_sem=send_sem,
        recv_sem=recv_sem,
        device_id=device,
        device_id_type=MESH,
    )


def pick(index, table):
    value = jnp.int32(table[0])
    for position, entry in enumerate(table[1:], 1):
        value = jnp.where(index == position, jnp.int32(entry), value)
    return value


def layer_kernel(
    feat,
    weight,
    table,
    labels,
    mask,
    vals,
    brow,
    bcol,
    bcnt,
    out,
    gw_out,
    gf_out,
    xv,
    vt,
    slots,
    part,
    zs,
    zr,
    ys,
    yr,
    keep,
    gath,
    gw32,
    gwb,
    gcr,
    gc32,
    gcb,
    g1r,
    g1t,
    g2r,
    g3,
    g4,
    sp,
    prx,
    chip,
    xs,
    xr,
    bs,
    br,
    bc_recv,
    bc_send,
    feed_send,
    z_send,
    z_recv,
    y_send,
    y_recv,
    ag_send,
    ag_recv,
    gw_send,
    gw_recv,
    p_send,
    p_recv,
    x_send,
    x_recv,
    b_send,
    b_recv,
):
    row = lax.axis_index("row")
    team = lax.axis_index("team")
    core = rem(row, 2)
    x = rem(div(row, 2), 4)
    ylo = div(row, 8)
    z = rem(team, 8)
    yhi = div(team, 8)

    def at_row(new_y, new_x, new_core):
        return ((new_y * 4 + rem(new_x + 4, 4)) * 2 + new_core, team)

    def at_team(new_yhi, new_z):
        return (row, new_yhi * 8 + rem(new_z + 8, 8))

    partner = at_row(ylo, x, 1 - core)
    x_up, x_down = at_row(ylo, x + 1, core), at_row(ylo, x - 1, core)
    y_side = at_row(1 - ylo, x, core)
    z_up, z_down = at_team(yhi, z + 1), at_team(yhi, z - 1)
    y_far = at_team(1 - yhi, z)

    barrier = pltpu.get_barrier_semaphore()

    def greet(d, carry):
        pl.semaphore_signal(
            barrier, inc=1, device_id=(rem(row + d, 16), team), device_id_type=MESH
        )
        pl.semaphore_signal(
            barrier, inc=1, device_id=(row, rem(team + d, 16)), device_id_type=MESH
        )
        return carry

    lax.fori_loop(1, 16, greet, 0)
    fed = (((1 - ylo) * 4 + x) * 2 + core, rem(team + 8, 16))
    pl.semaphore_signal(barrier, inc=1, device_id=fed, device_id_type=MESH)

    root = team
    root_core = rem(root, 2)
    rx = rem(x - rem(div(root, 2), 4) + 4, 4)
    ry = rem(ylo + div(root, 8), 2)
    lead = core == root_core
    is_root = row == root
    pieces = feat.shape[0] // PIECE

    def landed(piece):
        return xv.at[
            div(piece, 128 // PIECE),
            pl.ds(pl.multiple_of(rem(piece, 128 // PIECE) * PIECE, PIECE), PIECE),
        ]

    def stage(piece):
        return pltpu.make_async_copy(
            feat.at[pl.ds(pl.multiple_of(piece * PIECE, PIECE), PIECE)],
            landed(piece),
            bc_recv.at[piece],
        )

    @pl.when(is_root)
    def _():
        def begin(piece, carry):
            stage(piece).start()
            return carry

        lax.fori_loop(0, pieces, begin, 0)

    slots[16] = jnp.zeros((128, 512), F32)

    pl.semaphore_wait(barrier, 31)

    feeder = row == rem(team + 8, 16)

    def feed(piece):
        return remote(
            feat.at[pl.ds(pl.multiple_of(piece * PIECE, PIECE), PIECE)],
            landed(piece),
            feed_send.at[piece],
            bc_recv.at[piece],
            fed,
        )

    @pl.when(feeder)
    def _():
        def begin(q, carry):
            feed(q).start()

            @pl.when(q < TREES[1][1])
            def _():
                feed(TREES[1][0] + q).start()

            return carry

        lax.fori_loop(0, LONGEST, begin, 0)

    low = ry == 0
    depths = (
        jnp.where(low, pick(rx, (0, 1, 2, 3)), pick(rx, (3, 2, 3, 4))),
        jnp.where(low, pick(rx, (0, 3, 2, 1)), pick(rx, (3, 4, 3, 2))),
        jnp.where(low, pick(rx, (0, 3, 4, 3)), pick(rx, (1, 2, 3, 2))),
    )
    ups = (
        (low & (rx < 3)) | (~low & (rx == 2)),
        None,
        ~low & (rx < 2),
    )
    downs = (
        None,
        (low & (rx != 1)) | (~low & (rx > 1)),
        ~low & (rx == 0),
    )
    sides = (
        low & ((rx == 1) | (rx == 2)),
        low & (rx == 3),
        (low & (rx == 0)) | (~low & (rx > 0)),
    )

    def hop(piece, way, device):
        ref = landed(piece)
        return remote(ref, ref, bc_send.at[way, piece], bc_recv.at[piece], device)

    def branches(tree):
        return (
            (0, ups[tree], x_up),
            (1, downs[tree], x_down),
            (2, sides[tree], y_side),
            (3, None if tree < 0 else jnp.bool_(True), partner),
        )

    @pl.when(lead)
    def _():
        def beat(tick, carry):
            for tree, (first, number) in enumerate(TREES):
                q = tick - LAG * depths[tree]

                @pl.when((q >= 0) & (q < number))
                def _(tree=tree, first=first, q=q):
                    piece = first + q

                    @pl.when(is_root)
                    def _():
                        stage(piece).wait()

                    @pl.when(jnp.logical_not(is_root))
                    def _():
                        hop(piece, 3, partner).wait_recv()

                    for way, condition, device in branches(tree):
                        if condition is None:
                            continue

                        @pl.when(condition)
                        def _(way=way, device=device):
                            hop(piece, way, device).start()

            return carry

        lax.fori_loop(0, LONGEST + LAG * DEEPEST, beat, 0)

    @pl.when(jnp.logical_not(lead))
    def _():
        def arrive(piece, carry):
            hop(piece, 3, partner).wait_recv()
            return carry

        lax.fori_loop(0, pieces, arrive, 0)

    count = bcnt[0]

    def before(ids, k):
        found = jnp.int32(16)
        for other in range(k):
            found = jnp.where(ids[other] == ids[k], jnp.int32(other), found)
        return found

    def final(ids, target):
        found = jnp.int32(16)
        for other in range(16):
            hit = (ids[other] == target) & (jnp.int32(other) < count)
            found = jnp.where(hit, jnp.int32(other), found)
        return found

    for k in range(16):
        product = jnp.dot(vals[k], xv[bcol[k]], preferred_element_type=F32)
        slots[k] = product + slots[before(brow, k)] if k else product
    for s in range(16):
        value = slots[final(brow, s)].astype(BF16)
        for h in range(PARTS):
            part[h, s] = value[:, h * WIDE : (h + 1) * WIDE]

    def block(new_z, rel):
        return rem(yhi + rel, 2) * 8 + rem(new_z + 8, 8)

    ways = ((0, 1, z_up), (1, -1, z_down))

    def z_first(h, way, sign, device):
        return remote(
            part.at[h, block(z + 4, way)],
            zr.at[way, 0, h, way],
            z_send.at[way, 0, h],
            z_recv.at[way, 0, h],
            device,
        )

    def z_hop(h, way, step, device):
        return remote(
            zs.at[way, step, h],
            zr.at[way, step, h],
            z_send.at[way, step, h],
            z_recv.at[way, step, h],
            device,
        )

    for h in range(PARTS):
        for way, sign, device in ways:
            z_first(h, way, sign, device).start()

    for k in range(16):
        vt[k] = vals[k].T

    @pl.when(lead)
    def _():
        def settle(q, carry):
            for tree, (first, number) in enumerate(TREES):

                @pl.when(q < number)
                def _(tree=tree, first=first):
                    for way, condition, device in branches(tree):
                        if condition is None:
                            continue

                        @pl.when(condition)
                        def _(way=way, device=device):
                            hop(first + q, way, device).wait_send()

            return carry

        lax.fori_loop(0, LONGEST, settle, 0)

    @pl.when(feeder)
    def _():
        def fed_all(piece, carry):
            feed(piece).wait_send()
            return carry

        lax.fori_loop(0, FED, fed_all, 0)

    for step in range(1, 4):
        for h in range(PARTS):
            for way, sign, device in ways:
                if step == 1:
                    z_first(h, way, sign, device).wait_recv()
                else:
                    z_hop(h, way, step - 1, device).wait_recv()
                for rel in range(2):
                    value = part[h, block(z + sign * (4 - step), rel)]
                    if step > 1 or rel == way:
                        value = (
                            value.astype(F32) + zr[way, step - 1, h, rel].astype(F32)
                        ).astype(BF16)
                    zs[way, step, h, rel] = value
                z_hop(h, way, step, device).start()

    def y_hop(h):
        return remote(ys.at[h], yr.at[h], y_send.at[h], y_recv.at[h], y_far)

    for h in range(PARTS):
        for way, sign, device in ways:
            z_hop(h, way, 3, device).wait_recv()
        sums = [
            part[h, block(z, rel)].astype(F32)
            + zr[0, 3, h, rel].astype(F32)
            + zr[1, 3, h, rel].astype(F32)
            for rel in range(2)
        ]
        ys[h] = sums[1].astype(BF16)
        y_hop(h).start()
        keep[:, h * WIDE : (h + 1) * WIDE] = sums[0]
    for h in range(PARTS):
        y_hop(h).wait_recv()
    agg = jnp.concatenate(
        [
            (keep[:, h * WIDE : (h + 1) * WIDE] + yr[h].astype(F32)).astype(BF16)
            for h in range(PARTS)
        ],
        axis=1,
    )

    preact = jnp.dot(agg, weight[...], preferred_element_type=F32)
    sigma = jax.nn.sigmoid(preact)
    active = preact * sigma
    out[...] = active.astype(BF16)
    label_line = jnp.broadcast_to(labels[pl.ds(team, 1), :], (128, 128))
    classes = lax.broadcasted_iota(jnp.int32, (128, 128), 0)
    onehot = (label_line == classes).astype(F32).T
    spare = jnp.zeros((120, 512), F32)
    wide_table = jnp.concatenate([table[...].astype(F32), spare], axis=0)
    target = jnp.dot(onehot, wide_table, preferred_element_type=F32)
    known = jnp.broadcast_to(mask[pl.ds(team, 1), :], (128, 128)).astype(F32).T
    known = jnp.concatenate([known] * 4, axis=1)
    residual = known * (active - target)
    slope = sigma * (1.0 + preact * (1.0 - sigma))
    grad_pre = (residual * slope).astype(BF16)
    back = lax.dot_general(
        grad_pre, weight[...], (((1,), (1,)), ((), ())), preferred_element_type=F32
    ).astype(BF16)
    gath[team] = back

    def cols(h):
        return pl.ds(h * AG_WIDE, AG_WIDE)

    def ag_hop(step, way, rel, h, device):
        sign = 1 if way == 0 else -1
        origin = block(z - sign * (step - 1), rel)
        ref = gath.at[origin, :, cols(h)]
        return remote(
            ref, ref, ag_send.at[way, step, rel, h], ag_recv.at[way, step, rel, h], device
        )

    def ag_wait(step, way, rel, h, device):
        sign = 1 if way == 0 else -1
        origin = block(z - sign * step, rel)
        ref = gath.at[origin, :, cols(h)]
        remote(
            ref, ref, ag_send.at[way, step, rel, h], ag_recv.at[way, step, rel, h], device
        ).wait_recv()

    def ag_side(h, slot):
        ref = gath.at[slot, :, cols(h)]
        return remote(ref, ref, y_send.at[PARTS + h], y_recv.at[PARTS + h], y_far)

    def gw_pair():
        return remote(
            gwb.at[:, 1 - core], gcr, gw_send.at[0, 1], gw_recv.at[0, 1], partner
        )

    for h in range(AG_PARTS):
        ag_side(h, team).start()
        for way, sign, device in ways:
            ag_hop(1, way, 0, h, device).start()
    gw = lax.dot_general(
        agg, grad_pre, (((0,), (0,)), ((), ())), preferred_element_type=F32
    ).reshape(8, 2, 32, 512)
    gw32[...] = gw
    gwb[...] = gw.astype(BF16)
    gw_pair().start()

    def peer_row(d):
        return (rem(row + d, 16), team)

    def peer_team(d):
        return (row, rem(team + d, 16))

    def gw_hop(stage_id, d, receive):
        slot_row = rem(row - d + 16, 16) if receive else row
        slot_team = rem(team - d + 16, 16) if receive else team
        to_row, to_team = rem(row + d, 16), rem(team + d, 16)
        if stage_id == 0:
            src, dst, device = gcb.at[div(to_row, 2)], g1r.at[div(slot_row, 2)], peer_row(d)
        elif stage_id == 1:
            src, dst, device = g1t.at[to_team], g2r.at[slot_team], peer_team(d)
        elif stage_id == 2:
            src, dst, device = g3.at[slot_team], g3.at[slot_team], peer_team(d)
        else:
            spot = g4.at[div(slot_row, 2), rem(slot_row, 2)]
            src, dst, device = spot, spot, peer_row(d)
        return remote(
            src, dst, gw_send.at[stage_id, d], gw_recv.at[stage_id, d], device
        )

    def peers(stage_id):
        return range(2, 16, 2) if stage_id in (0, 3) else range(1, 16)

    def gw_start(stage_id):
        for d in peers(stage_id):
            gw_hop(stage_id, d, False).start()

    def gw_arrive(stage_id):
        for d in peers(stage_id):
            gw_hop(stage_id, d, True).wait_recv()

    def gw_chip():
        gw_pair().wait_recv()
        for m in range(8):
            both = gw32[m, core] + gcr[m].astype(F32)
            gc32[m] = both
            gcb[m] = both.astype(BF16)
        gw_start(0)

    def gw_stage(stage_id):
        gw_arrive(stage_id)
        if stage_id == 0:

            total = gc32[div(row, 2)]
            for d in range(1, 8):
                total = total + g1r[rem(div(row, 2) + d, 8)].astype(F32)
            for a in range(4):
                for b in range(4):
                    g1t[a * 4 + b] = total[a * 8 : a * 8 + 8, b * 128 : b * 128 + 128]
        elif stage_id == 1:

            total = g1t[team]
            for d in range(1, 16):
                total = total + g2r[rem(team + d, 16)]
            g3[team] = total
        elif stage_id == 2:
            lines = [
                jnp.concatenate([g3[a * 4 + b] for b in range(4)], axis=1)
                for a in range(4)
            ]
            scale = 1.0 / math.sqrt(32768)
            g4[div(row, 2), core] = (jnp.concatenate(lines, axis=0) * scale).astype(BF16)
        gw_start(stage_id + 1)

    def gw_across(receive):
        side = g4.at[:, 1 - core if receive else core]
        return remote(side, side, gw_send.at[3, 1], gw_recv.at[3, 1], partner)

    for h in range(PARTS):
        for way, sign, device in ways:
            z_first(h, way, sign, device).wait_send()
            for step in range(1, 4):
                z_hop(h, way, step, device).wait_send()
        y_hop(h).wait_send()
    for tick in range(2, 6):
        for rel in range(2):
            step = tick - rel
            if step > 4:
                continue
            for h in range(AG_PARTS):
                if step == 1:
                    ag_side(h, rem(team + 8, 16)).wait_recv()
                for way, sign, device in ways:
                    if step > 1:
                        ag_wait(step - 1, way, rel, h, device)
                    if step < 4 or rel == way:
                        ag_hop(step, way, rel, h, device).start()
        if tick == 2:
            gw_chip()
        elif tick == 4:
            gw_stage(0)
    for rel in range(2):
        for h in range(AG_PARTS):
            ag_wait(4, rel, rel, h, ways[rel][2])
    gw_stage(1)

    for k in range(16):
        product = jnp.dot(vt[k], gath[brow[k]], preferred_element_type=F32)
        slots[k] = product + slots[before(bcol, k)] if k else product
    for s in range(16):
        value = slots[final(bcol, s)].astype(BF16)
        for h in range(PARTS):
            sp[h, s % 2, s // 2] = value[:, h * WIDE : (h + 1) * WIDE]

    def p_hop(h):
        return remote(sp.at[h, 1 - core], prx.at[h], p_send.at[h], p_recv.at[h], partner)

    def chip_block(new_x, rel):
        return rem(ylo + rel, 2) * 4 + rem(new_x + 4, 4)

    x_ways = ((0, 1, x_up), (1, -1, x_down))

    def x_first(h, way, device):
        return remote(
            chip.at[h, chip_block(x + 2, way)],
            xr.at[way, 0, h, way],
            x_send.at[way, 0, h],
            x_recv.at[way, 0, h],
            device,
        )

    def x_hop(h, way, device):
        return remote(
            xs.at[way, h],
            xr.at[way, 1, h],
            x_send.at[way, 1, h],
            x_recv.at[way, 1, h],
            device,
        )

    def b_hop(h):
        return remote(bs.at[h], br.at[h], b_send.at[h], b_recv.at[h], y_side)

    for h in range(PARTS):
        p_hop(h).start()
    gw_stage(2)
    for h in range(PARTS):
        p_hop(h).wait_recv()

        def fold(m, carry, h=h):
            chip[h, m] = (sp[h, core, m].astype(F32) + prx[h, m].astype(F32)).astype(BF16)
            return carry

        lax.fori_loop(0, 8, fold, 0)
        for way, sign, device in x_ways:
            x_first(h, way, device).start()
    for h in range(AG_PARTS):
        ag_side(h, team).wait_send()
        for way, sign, device in ways:
            for rel in range(2):
                for step in range(1, 5):
                    if step < 4 or rel == way:
                        ag_hop(step, way, rel, h, device).wait_send()

    gw_pair().wait_send()
    for stage_id in range(3):
        for d in peers(stage_id):
            gw_hop(stage_id, d, False).wait_send()
    for h in range(PARTS):
        for way, sign, device in x_ways:
            x_first(h, way, device).wait_recv()
            for rel in range(2):
                value = chip[h, chip_block(x + sign, rel)]
                if rel == way:
                    value = (value.astype(F32) + xr[way, 0, h, rel].astype(F32)).astype(BF16)
                xs[way, h, rel] = value
            x_hop(h, way, device).start()
    for h in range(PARTS):
        for way, sign, device in x_ways:
            x_hop(h, way, device).wait_recv()
        sums = [
            chip[h, chip_block(x, rel)].astype(F32)
            + xr[0, 1, h, rel].astype(F32)
            + xr[1, 1, h, rel].astype(F32)
            for rel in range(2)
        ]
        bs[h] = sums[1].astype(BF16)
        b_hop(h).start()
        keep[:, h * WIDE : (h + 1) * WIDE] = sums[0]
    gw_arrive(3)
    gw_across(False).start()
    for h in range(PARTS):
        b_hop(h).wait_recv()
        gf_out[:, h * WIDE : (h + 1) * WIDE] = (
            keep[:, h * WIDE : (h + 1) * WIDE] + br[h].astype(F32)
        ).astype(BF16)

    gw_across(True).wait_recv()
    gw_out[...] = g4[...].reshape(16, 32, 512)
    for d in peers(3):
        gw_hop(3, d, False).wait_send()
    gw_across(False).wait_send()
    for h in range(PARTS):
        p_hop(h).wait_send()
        b_hop(h).wait_send()
        for way, sign, device in x_ways:
            x_first(h, way, device).wait_send()
            x_hop(h, way, device).wait_send()


def per_device(
    features, weight, table, labels, label_mask, block_vals, block_row, block_col, block_count
):
    vmem = pl.BlockSpec(memory_space=pltpu.VMEM)
    smem = pl.BlockSpec(memory_space=pltpu.SMEM)
    dma = pltpu.SemaphoreType.DMA
    half = (PARTS, 128, WIDE)
    outs = pl.pallas_call(
        layer_kernel,
        out_shape=(
            jax.ShapeDtypeStruct((128, 512), BF16),
            jax.ShapeDtypeStruct((16, 32, 512), BF16),
            jax.ShapeDtypeStruct((128, 512), BF16),
        ),
        in_specs=[pl.BlockSpec(memory_space=pl.ANY)] + [vmem] * 5 + [smem] * 3,
        out_specs=(vmem, vmem, vmem),
        scratch_shapes=[
            pltpu.VMEM((16, 128, 512), BF16),
            pltpu.VMEM((16, 128, 128), BF16),
            pltpu.VMEM((17, 128, 512), F32),
            pltpu.VMEM((PARTS, 16, 128, WIDE), BF16),
            pltpu.VMEM((2, 4, PARTS, 2, 128, WIDE), BF16),
            pltpu.VMEM((2, 4, PARTS, 2, 128, WIDE), BF16),
            pltpu.VMEM(half, BF16),
            pltpu.VMEM(half, BF16),
            pltpu.VMEM((128, 512), F32),
            pltpu.VMEM((16, 128, 512), BF16),
            pltpu.VMEM((8, 2, 32, 512), F32),
            pltpu.VMEM((8, 2, 32, 512), BF16),
            pltpu.VMEM((8, 32, 512), BF16),
            pltpu.VMEM((8, 32, 512), F32),
            pltpu.VMEM((8, 32, 512), BF16),
            pltpu.VMEM((8, 32, 512), BF16),
            pltpu.VMEM((16, 8, 128), F32),
            pltpu.VMEM((16, 8, 128), F32),
            pltpu.VMEM((16, 8, 128), F32),
            pltpu.VMEM((8, 2, 32, 512), BF16),
            pltpu.VMEM((PARTS, 2, 8, 128, WIDE), BF16),
            pltpu.VMEM((PARTS, 8, 128, WIDE), BF16),
            pltpu.VMEM((PARTS, 8, 128, WIDE), BF16),
            pltpu.VMEM((2, PARTS, 2, 128, WIDE), BF16),
            pltpu.VMEM((2, 2, PARTS, 2, 128, WIDE), BF16),
            pltpu.VMEM(half, BF16),
            pltpu.VMEM(half, BF16),
            dma((64,)),
            dma((4, 64)),
            dma((64,)),
            dma((2, 4, PARTS)),
            dma((2, 4, PARTS)),
            dma((PARTS + AG_PARTS,)),
            dma((PARTS + AG_PARTS,)),
            dma((2, 5, 2, AG_PARTS)),
            dma((2, 5, 2, AG_PARTS)),
            dma((4, 16)),
            dma((4, 16)),
            dma((PARTS,)),
            dma((PARTS,)),
            dma((2, 2, PARTS)),
            dma((2, 2, PARTS)),
            dma((PARTS,)),
            dma((PARTS,)),
        ],
        compiler_params=pltpu.CompilerParams(collective_id=0, has_side_effects=True),
        name="layer",
    )(
        features,
        weight,
        table,
        labels.reshape(16, 128),
        label_mask.reshape(16, 128),
        block_vals[0, 0],
        block_row[0, 0],
        block_col[0, 0],
        block_count[0],
    )
    output, grad_weight, grad_piece = outs
    return (output, grad_weight.reshape(512, 512).astype(F32), grad_piece[None])


def solution(mesh):
    placed = (
        P("row", None),
        P(),
        P(),
        P("row"),
        P("row"),
        P("row", "team", None, None, None),
        P("row", "team", None),
        P("row", "team", None),
        P("row", "team"),
    )
    return jax.shard_map(
        per_device,
        mesh=mesh,
        in_specs=placed,
        out_specs=(P(("row", "team"), None), P(), P("team", "row", None)),
        check_vma=False,
    )
```
